256 devices in a mesh: store: 16 (over y, x_hi, core), dept: 16 (over z, x_lo).
Axes of the slice: x: 4 (x_hi: 2, x_lo: 2; x = x_hi * 2 + x_lo), y: 4, z: 8, core: 2. Of those that a mesh axis runs over, the one named last changes fastest.
Arguments:
- history: bfloat16 [4096, 384, 512], P('store', 'dept'), may hold values from -400 to 400, as said below
- input_layer_matrix: bfloat16 [512, 512], replicated, may hold values from -0.375 to 0.375
- middle_layer_matrix: bfloat16 [512, 512], replicated, may hold values from -0.375 to 0.375
- final_layer_matrix: bfloat16 [512, 28], replicated, may hold values from -0.375 to 0.375
Outputs:
- reconciled: float32 [4096, 10752], P('store', 'dept')
- store_gap: float32 [28, 4096], P(None, 'store')
- item_gap: float32 [28, 384], P(None, 'dept')
The draws below stay inside these ranges and needn't reach their ends.
Inputs may be any that keep to these rules, and one draw needn't show every extreme that they name: `history`: daily sales histories.
All inputs are finite; a program needn't handle non-finite values.
Results may differ from the reference program's by a relative error of at most 0.0065.
The reference program's roundings to bfloat16 on the way count: a program that leaves them out, or rounds other values in their place, can miss the bound.
Values sent between devices are 32-bit elements; how exact they have to be, the bound alone decides.
No kernel may reach another device: no remote copies, remote signals or barrier semaphores. Data moves between devices by JAX's collectives and lax.ppermute only.
A program may use at most 64 MiB of HBM per device.

```python
import math
import jax
import jax.numpy as jnp
from jax import lax

OUTLETS_IN_PIECE = 256
PAST_LENGTH = 512
HID = 512
AHEAD_LENGTH = 28
STORES = 4096
PRODUCT_NUMBER = 384


def draw_history(key, part):
    subkeys = jax.random.split(key, 4)
    store_scale = jnp.exp(jax.random.uniform(subkeys[0], (STORES,), jnp.float32, -1.15, 1.15))
    store_scale = store_scale * 3.0 ** (jnp.arange(STORES, dtype=jnp.float32) / STORES)
    item_scale = jnp.exp(jax.random.uniform(subkeys[1], (PRODUCT_NUMBER,), jnp.float32, -0.7, 0.7))
    item_scale = item_scale * 3.0 ** (jnp.arange(PRODUCT_NUMBER, dtype=jnp.float32) / PRODUCT_NUMBER)
    day_scale = jnp.exp(jax.random.uniform(subkeys[2], (PAST_LENGTH,), jnp.float32, -1.15, 1.15))
    jitter = jnp.clip(jax.random.normal(subkeys[3], (STORES, PRODUCT_NUMBER, PAST_LENGTH), jnp.float32), -4.0, 4.0)
    scaled = 0.3 * store_scale[:, None, None] * item_scale[None, :, None] * day_scale[None, None, :] * jitter
    return scaled.astype(jnp.bfloat16)


def scatter_about(rng, dims, width, limit, held_as=jnp.bfloat16):
    result = width * jax.random.normal(rng, dims, jnp.float32)
    return jnp.clip(result, min=-limit, max=limit).astype(held_as)


def setup_inputs(seed: int = 0) -> dict:
    key_list = jax.random.split(jax.random.key(seed), 5)
    history = draw_history(jax.random.fold_in(key_list[4], 71), 0)
    input_layer_matrix = scatter_about(key_list[1], (PAST_LENGTH, HID), (PAST_LENGTH // 2) ** -0.5, 0.375)
    middle_layer_matrix = scatter_about(key_list[2], (HID, HID), (HID // 2) ** -0.5, 0.375)
    final_layer_matrix = scatter_about(key_list[3], (HID, AHEAD_LENGTH), (HID // 2) ** -0.5, 0.375)
    return {"history": history, "input_layer_matrix": input_layer_matrix, "middle_layer_matrix": middle_layer_matrix, "final_layer_matrix": final_layer_matrix}


def predictor_function(sequence_grid, input_layer_matrix, middle_layer_matrix, final_layer_matrix):
    values = sequence_grid.astype(jnp.float32)
    root_mean = jnp.sqrt(lax.optimization_barrier(jnp.mean(values * values, axis=-1, keepdims=True)) + 1e-05)
    scaled = (values / root_mean).astype(jnp.bfloat16)
    hidden_one = jax.nn.relu(jnp.dot(scaled, input_layer_matrix, preferred_element_type=jnp.float32)).astype(jnp.bfloat16)
    hidden_two = jax.nn.relu(jnp.dot(hidden_one, middle_layer_matrix, preferred_element_type=jnp.float32)).astype(jnp.bfloat16)
    return jnp.dot(hidden_two, final_layer_matrix, preferred_element_type=jnp.float32) * root_mean

def reference(history, input_layer_matrix, middle_layer_matrix, final_layer_matrix):
    blocks = history.reshape(-1, OUTLETS_IN_PIECE, PRODUCT_NUMBER, PAST_LENGTH)

    def per_block(outlet_portion):
        projected_grid = predictor_function(outlet_portion.reshape(-1, PAST_LENGTH), input_layer_matrix, middle_layer_matrix, final_layer_matrix).reshape(OUTLETS_IN_PIECE, PRODUCT_NUMBER, AHEAD_LENGTH)
        widened_entries = outlet_portion.astype(jnp.float32)
        return (projected_grid, lax.optimization_barrier(jnp.sum(widened_entries, axis=1)), lax.optimization_barrier(jnp.sum(widened_entries, axis=0)))
    finest_tier, outlet_past_sales, item_parts = lax.map(per_block, blocks)
    finest_tier = finest_tier.reshape(STORES, PRODUCT_NUMBER, AHEAD_LENGTH)
    outlet_past_sales = outlet_past_sales.reshape(STORES, PAST_LENGTH)
    product_past_sales = lax.optimization_barrier(jnp.sum(item_parts, axis=0))
    outlet_estimate = predictor_function(outlet_past_sales, input_layer_matrix, middle_layer_matrix, final_layer_matrix)
    product_estimate = predictor_function(product_past_sales, input_layer_matrix, middle_layer_matrix, final_layer_matrix)
    row_sum = lax.optimization_barrier(jnp.sum(finest_tier, axis=1))
    col_sum = lax.optimization_barrier(jnp.sum(finest_tier, axis=0))
    store_err = outlet_estimate - row_sum
    item_err = product_estimate - col_sum
    err_s = lax.optimization_barrier(jnp.sum(store_err, axis=0))
    err_i = lax.optimization_barrier(jnp.sum(item_err, axis=0))
    item_count = float(PRODUCT_NUMBER)
    store_count = float(STORES)
    denominator = 1.0 + item_count + store_count
    shift_s = (err_s * (1.0 + store_count) - store_count * err_i) / denominator
    shift_i = ((1.0 + item_count) * err_i - item_count * err_s) / denominator
    store_shift = (store_err - shift_i) / (1.0 + item_count)
    item_shift = (item_err - shift_s) / (1.0 + store_count)
    reconciled = finest_tier + store_shift[:, None, :] + item_shift[None, :, :]
    store_gap = (store_err / math.sqrt(item_count)).T
    item_gap = (item_err / math.sqrt(store_count)).T
    return (reconciled.reshape(STORES, PRODUCT_NUMBER * AHEAD_LENGTH), store_gap, item_gap)
```

```python
import functools
import math

import jax
import jax.numpy as jnp
from jax import lax
from jax.experimental import pallas as pl
from jax.experimental.pallas import tpu as pltpu
from jax.sharding import PartitionSpec as P

F32 = jnp.float32
BF16 = jnp.bfloat16
LANES = 128
GROUP = 32
VMEM_LIMIT = 50 * 1024 * 1024


def whole(n):
    return [pl.BlockSpec(memory_space=pltpu.VMEM)] * n


def params(semantics=None):
    return pltpu.CompilerParams(
        dimension_semantics=semantics, vmem_limit_bytes=VMEM_LIMIT
    )


def forecaster(x, w1, w2, w3):
    var = jnp.sum(x * x, axis=-1, keepdims=True) * (1.0 / x.shape[-1]) + 1e-05
    inv = lax.rsqrt(var)
    z = (x * inv).astype(BF16)
    a = jnp.maximum(jnp.dot(z, w1, preferred_element_type=F32), 0.0).astype(BF16)
    b = jnp.maximum(jnp.dot(a, w2, preferred_element_type=F32), 0.0).astype(BF16)
    return jnp.dot(b, w3, preferred_element_type=F32) * (var * inv)


def sums_kernel(h_ref, store_ref, item_ref):
    x = h_ref[...].astype(F32)
    store_ref[...] = jnp.sum(x, axis=1)

    @pl.when(pl.program_id(0) == 0)
    def _():
        item_ref[...] = jnp.zeros_like(item_ref)

    item_ref[: x.shape[1], :] += jnp.sum(x, axis=0)


def history_sums(history, item_rows, block):
    stores, items, days = history.shape
    return pl.pallas_call(
        sums_kernel,
        grid=(stores // block,),
        in_specs=[pl.BlockSpec((block, items, days), lambda i: (i, 0, 0))],
        out_specs=[
            pl.BlockSpec((block, days), lambda i: (i, 0)),
            pl.BlockSpec((item_rows, days), lambda i: (0, 0)),
        ],
        out_shape=[
            jax.ShapeDtypeStruct((stores, days), F32),
            jax.ShapeDtypeStruct((item_rows, days), F32),
        ],
        compiler_params=params(("arbitrary",)),
        cost_estimate=pl.CostEstimate(
            flops=2 * history.size, bytes_accessed=2 * history.size, transcendentals=0
        ),
        name="history_sums",
    )(history)


def base_kernel(horizon, part, h_ref, w1_ref, w2_ref, w3_ref, base_ref, row_ref, col_ref, y_ref):
    block, items, days = h_ref.shape
    w1, w2, w3 = w1_ref[...], w2_ref[...], w3_ref[...]
    for p in range(block // part):
        x = h_ref[p * part : (p + 1) * part].astype(F32).reshape(part * items, days)
        y_ref[p * part * items : (p + 1) * part * items, :] = forecaster(x, w1, w2, w3)
    y = y_ref[...].reshape(block, items, LANES)
    row_ref[...] = jnp.sum(y, axis=1)

    @pl.when(pl.program_id(0) == 0)
    def _():
        col_ref[...] = jnp.zeros_like(col_ref)

    col_ref[...] += jnp.sum(y, axis=0)
    lane = lax.broadcasted_iota(jnp.int32, (block, LANES), 1)
    tiles = [None] * pl.cdiv(items * horizon, LANES)

    def add(t, v):
        tiles[t] = v if tiles[t] is None else tiles[t] + v

    for i in range(items):
        v = y_ref[pl.ds(i, block, stride=items), :]
        t, off = divmod(i * horizon, LANES)
        if off:
            v = pltpu.roll(v, off, axis=1)
        if off + horizon > LANES:
            add(t, jnp.where(lane >= off, v, 0.0))
            add(t + 1, jnp.where(lane < off, v, 0.0))
        else:
            add(t, v)
    for t, v in enumerate(tiles):
        width = min(LANES, items * horizon - t * LANES)
        base_ref[:, t * LANES : t * LANES + width] = v[:, :width]


def base_forecasts(history, w1, w2, w3, horizon, block, part):
    stores, items, days = history.shape
    hid = w1.shape[1]
    rows = stores * items
    fixed = lambda shape: pl.BlockSpec(shape, lambda i: (0, 0))
    return pl.pallas_call(
        functools.partial(base_kernel, horizon, part),
        grid=(stores // block,),
        in_specs=[
            pl.BlockSpec((block, items, days), lambda i: (i, 0, 0)),
            fixed(w1.shape),
            fixed(w2.shape),
            fixed(w3.shape),
        ],
        out_specs=[
            pl.BlockSpec((block, items * horizon), lambda i: (i, 0)),
            pl.BlockSpec((block, LANES), lambda i: (i, 0)),
            fixed((items, LANES)),
        ],
        out_shape=[
            jax.ShapeDtypeStruct((stores, items * horizon), F32),
            jax.ShapeDtypeStruct((stores, LANES), F32),
            jax.ShapeDtypeStruct((items, LANES), F32),
        ],
        scratch_shapes=[pltpu.VMEM((block * items, LANES), F32)],
        compiler_params=params(("arbitrary",)),
        cost_estimate=pl.CostEstimate(
            flops=2 * rows * (days * hid + hid * hid + hid * LANES),
            bytes_accessed=2 * history.size + 4 * stores * items * horizon,
            transcendentals=0,
        ),
        name="base_forecasts",
    )(history, w1, w2, w3)


def totals_kernel(s_ref, i_ref, w1_ref, w2_ref, w3_ref, col_ref, fc_ref, pay_ref):
    peers, chunk, days = s_ref.shape
    per = i_ref.shape[1]
    xs = s_ref[0]
    xi = i_ref[0]
    for p in range(1, peers):
        xs = xs + s_ref[p]
        xi = xi + i_ref[p]
    pad = jnp.zeros((8 - per, days), F32)
    x = jnp.concatenate([xs, xi, pad], axis=0)
    y = forecaster(x, w1_ref[...], w2_ref[...], w3_ref[...])
    fc = y[:chunk]
    fi = y[chunk : chunk + per]
    fc_ref[...] = fc
    col = col_ref[...]
    sums = (
        jnp.sum(fc, axis=0, keepdims=True)
        + pltpu.roll(jnp.sum(fi, axis=0, keepdims=True), GROUP, axis=1)
        + pltpu.roll(jnp.sum(col, axis=0, keepdims=True), 2 * GROUP, axis=1)
    )
    forecasts = fi[0:1]
    for k in range(1, per):
        forecasts = forecasts + pltpu.roll(fi[k : k + 1], k * GROUP, axis=1)
    n = col.shape[0] // 4
    packed = col[0:n]
    for k in range(1, 4):
        packed = packed + pltpu.roll(col[k * n : (k + 1) * n], k * GROUP, axis=1)
    for p in range(peers):
        pay_ref[p, 0:n, :] = packed
        pay_ref[p, n : n + 1, :] = sums
        pay_ref[p, n + 1 : n + 2, :] = forecasts


def totals(store_parts, item_parts, w1, w2, w3, col):
    peers, chunk, _ = store_parts.shape
    return pl.pallas_call(
        totals_kernel,
        in_specs=whole(6),
        out_specs=whole(2),
        out_shape=[
            jax.ShapeDtypeStruct((chunk, LANES), F32),
            jax.ShapeDtypeStruct((peers, 8, LANES), F32),
        ],
        compiler_params=params(),
        name="totals",
    )(store_parts, item_parts, w1, w2, w3, col)


def middle_kernel(fc_ref, row_ref, got_ref, pay_ref):
    peers, chunk, _ = row_ref.shape
    row = row_ref[0]
    for p in range(1, peers):
        row = row + row_ref[p]
    n = 6
    sums = got_ref[0, n : n + 1, :]
    for p in range(1, got_ref.shape[0]):
        sums = sums + got_ref[p, n : n + 1, :]
    err = fc_ref[...] - row
    q = chunk // 4
    packed = err[0:q]
    for k in range(1, 4):
        packed = packed + pltpu.roll(err[k * q : (k + 1) * q], k * GROUP, axis=1)
    for p in range(peers):
        pay_ref[p, 0:q, :] = packed
        pay_ref[p, q : q + 1, :] = sums


def middle(fc, row_parts, got):
    peers = row_parts.shape[0]
    return pl.pallas_call(
        middle_kernel,
        in_specs=whole(3),
        out_specs=whole(1)[0],
        out_shape=jax.ShapeDtypeStruct((peers, 8, LANES), F32),
        compiler_params=params(),
        name="middle",
    )(fc, row_parts, got)


def final_kernel(horizon, item_count, store_count, base_ref, one_ref, two_ref, out_ref, sgap_ref, igap_ref, err_ref):
    stores, width = base_ref.shape
    items = width // horizon
    peers = two_ref.shape[0]
    lane1 = lax.broadcasted_iota(jnp.int32, (1, LANES), 1)
    valid1 = lane1 < horizon

    n = items // 4
    per = items // (items // 2)
    colp = one_ref[0, 0:n, :]
    for p in range(1, one_ref.shape[0]):
        colp = colp + one_ref[p, 0:n, :]
    groups = []
    for k in range(4):
        g = colp if k == 0 else pltpu.roll(colp, LANES - k * GROUP, axis=1)
        groups.append(jnp.where(valid1, g, 0.0))
    col = jnp.concatenate(groups, axis=0)
    rows = []
    for i in range(items):
        p, k = divmod(i, per)
        g = one_ref[p, n + 1 : n + 2, :]
        if k:
            g = pltpu.roll(g, LANES - k * GROUP, axis=1)
        rows.append(jnp.where(valid1, g, 0.0))
    item_err = jnp.concatenate(rows, axis=0) - col

    q = stores // peers // 4
    sums = two_ref[0, q : q + 1, :]
    for p in range(1, peers):
        sums = sums + two_ref[p, q : q + 1, :]
    total = pltpu.roll(sums, LANES - 2 * GROUP, axis=1)
    err_s = jnp.where(valid1, sums - total, 0.0)
    err_i = jnp.where(valid1, pltpu.roll(sums, LANES - GROUP, axis=1) - total, 0.0)
    for k in range(4):
        for p in range(peers):
            g = two_ref[p, 0:q, :]
            if k:
                g = pltpu.roll(g, LANES - k * GROUP, axis=1)
            r = p * 4 * q + k * q
            err_ref[r : r + q, :] = jnp.where(valid1, g, 0.0)
    store_err = err_ref[...]

    denominator = 1.0 + item_count + store_count
    shift_s = (err_s * (1.0 + store_count) - store_count * err_i) / denominator
    shift_i = ((1.0 + item_count) * err_i - item_count * err_s) / denominator
    store_shift = (store_err - shift_i) / (1.0 + item_count)
    item_shift = (item_err - shift_s) / (1.0 + store_count)

    day = lax.broadcasted_iota(jnp.int32, (LANES, LANES), 0)
    lane = lax.broadcasted_iota(jnp.int32, (LANES, LANES), 1)
    which = lax.broadcasted_iota(jnp.int32, (items, LANES), 0)
    lane_i = lax.broadcasted_iota(jnp.int32, (items, LANES), 1)
    for t in range(pl.cdiv(width, LANES)):
        first = (t * LANES) // horizon
        place = lane + (t * LANES - first * horizon) - day
        one_hot = jnp.zeros((LANES, LANES), F32)
        for m in range(LANES // horizon + 2):
            one_hot = jnp.where((place == m * horizon) & (day < horizon), 1.0, one_hot)
        spread = functools.partial(
            jnp.dot, precision=lax.Precision.HIGHEST, preferred_element_type=F32
        )
        a = spread(store_shift, one_hot)
        b = spread(item_shift, one_hot)
        pos = lane_i + t * LANES - which * horizon
        b = jnp.sum(jnp.where((pos >= 0) & (pos < horizon), b, 0.0), axis=0, keepdims=True)
        w = min(LANES, width - t * LANES)
        out_ref[:, t * LANES : t * LANES + w] = (
            base_ref[:, t * LANES : t * LANES + w] + a[:, :w] + b[:, :w]
        )
    sgap_ref[...] = (store_err * (1.0 / math.sqrt(item_count))).T[:horizon, :]
    padded = jnp.concatenate([item_err, jnp.zeros((LANES - items, LANES), F32)], axis=0)
    igap_ref[...] = (padded * (1.0 / math.sqrt(store_count))).T[:horizon, :items]


def final(base, one, two, horizon, item_count, store_count):
    stores, width = base.shape
    items = width // horizon
    return pl.pallas_call(
        functools.partial(final_kernel, horizon, item_count, store_count),
        in_specs=whole(3),
        out_specs=whole(3),
        out_shape=[
            jax.ShapeDtypeStruct((stores, width), F32),
            jax.ShapeDtypeStruct((horizon, stores), F32),
            jax.ShapeDtypeStruct((horizon, items), F32),
        ],
        scratch_shapes=[pltpu.VMEM((stores, LANES), F32)],
        compiler_params=params(),
        name="final",
    )(base, one, two)


def exchange(x, axis):
    return lax.all_to_all(x, axis, 0, 0, tiled=True)


def body(history, w1, w2, final_layer_matrix):
    stores, items, days = history.shape
    horizon = final_layer_matrix.shape[1]
    n_store, n_dept = lax.axis_size("store"), lax.axis_size("dept")
    per = pl.cdiv(items, n_store)
    w3 = jnp.pad(final_layer_matrix, ((0, 0), (0, LANES - horizon)))

    store_part, item_part = history_sums(history, per * n_store, 32)
    store_parts = exchange(store_part.reshape(n_dept, stores // n_dept, days), "dept")
    item_parts = exchange(item_part.reshape(n_store, per, days), "store")
    base, row_part, col_part = base_forecasts(history, w1, w2, w3, horizon, 32, 8)
    row_parts = exchange(row_part.reshape(n_dept, stores // n_dept, LANES), "dept")
    fc, pay_one = totals(store_parts, item_parts, w1, w2, w3, col_part)
    one = exchange(pay_one, "store")
    pay_two = middle(fc, row_parts, one)
    two = exchange(pay_two, "dept")
    return final(base, one, two, horizon, float(items * n_dept), float(stores * n_store))


def solution(mesh):
    return jax.shard_map(
        body,
        mesh=mesh,
        in_specs=(P("store", "dept", None), P(), P(), P()),
        out_specs=(P("store", "dept"), P(None, "store"), P(None, "dept")),
        check_vma=False,
    )
```

```python
import functools
import math

import jax
import jax.numpy as jnp
from jax import lax
from jax.experimental import pallas as pl
from jax.experimental.pallas import tpu as pltpu
from jax.sharding import PartitionSpec as P

F32 = jnp.float32
BF16 = jnp.bfloat16
LANES = 128
GROUP = 32
VMEM_LIMIT = 50 * 1024 * 1024


def whole(n):
    return [pl.BlockSpec(memory_space=pltpu.VMEM)] * n


def params(semantics=None, limit=VMEM_LIMIT):
    return pltpu.CompilerParams(dimension_semantics=semantics, vmem_limit_bytes=limit)


def relu(x):
    return jnp.maximum(x.astype(BF16), 0)


def forecaster(x, w1, w2, w3):
    var = jnp.sum(x * x, axis=-1, keepdims=True) * (1.0 / x.shape[-1]) + 1e-05
    inv = lax.rsqrt(var)
    z = (x * inv).astype(BF16)
    a = relu(jnp.dot(z, w1, preferred_element_type=F32))
    b = relu(jnp.dot(a, w2, preferred_element_type=F32))
    return jnp.dot(b, w3, preferred_element_type=F32) * (var * inv)


def widen(w3_ref, w3_wide):
    horizon = w3_ref.shape[0]
    w3_wide[...] = jnp.zeros_like(w3_wide)
    w3_wide[:, :horizon] = w3_ref[...].astype(F32).T.astype(BF16)


def pack_rows(x):
    n = x.shape[0] // 4
    out = x[0:n]
    for k in range(1, 4):
        out = out + pltpu.roll(x[k * n : (k + 1) * n], k * GROUP, axis=1)
    return out


def bottom_kernel(chunk, part, h_ref, w1_ref, w2_ref, w3_ref, pay_ref, item_ref, col_ref, y_ref, w3_wide):
    block, items, days = h_ref.shape
    step = pl.program_id(0)

    @pl.when(step == 0)
    def _():
        widen(w3_ref, w3_wide)
        item_ref[...] = jnp.zeros_like(item_ref)
        col_ref[...] = jnp.zeros_like(col_ref)

    w1, w2, w3 = w1_ref[...], w2_ref[...], w3_wide[...]
    tiles = days // LANES
    for p in range(block // part):
        x = h_ref[p * part : (p + 1) * part].astype(F32)
        by_store = jnp.sum(x, axis=1)
        item_ref[...] += jnp.sum(x, axis=0)
        y = forecaster(x.reshape(part * items, days), w1, w2, w3)
        y_ref[p * part * items : (p + 1) * part * items, :] = y
        y = y.reshape(part, items, LANES)
        row = jnp.sum(y, axis=1)
        col_ref[...] += jnp.sum(y, axis=0)
        for q in range(part // chunk):
            peer = p * (part // chunk) + q
            for t in range(tiles):
                pay_ref[peer, t * chunk : (t + 1) * chunk, :] = by_store[
                    q * chunk : (q + 1) * chunk, t * LANES : (t + 1) * LANES
                ]
            pay_ref[peer, tiles * chunk : tiles * chunk + chunk // 4, :] = pack_rows(
                row[q * chunk : (q + 1) * chunk]
            )


def bottom(history, w1, w2, w3, peers, block, part):
    stores, items, days = history.shape
    hid = w1.shape[1]
    rows = stores * items
    chunk = stores // peers
    pay_rows = (days // LANES) * chunk + 8
    fixed = lambda shape: pl.BlockSpec(shape, lambda i: (0,) * len(shape))
    return pl.pallas_call(
        functools.partial(bottom_kernel, chunk, part),
        grid=(stores // block,),
        in_specs=[
            pl.BlockSpec((block, items, days), lambda i: (i, 0, 0)),
            fixed(w1.shape),
            fixed(w2.shape),
            fixed(w3.shape),
        ],
        out_specs=[
            pl.BlockSpec((block // chunk, pay_rows, LANES), lambda i: (i, 0, 0)),
            fixed((items, days)),
            fixed((items, LANES)),
            pl.BlockSpec((block * items, LANES), lambda i: (i, 0)),
        ],
        out_shape=[
            jax.ShapeDtypeStruct((peers, pay_rows, LANES), F32),
            jax.ShapeDtypeStruct((items, days), F32),
            jax.ShapeDtypeStruct((items, LANES), F32),
            jax.ShapeDtypeStruct((rows, LANES), F32),
        ],
        scratch_shapes=[pltpu.VMEM((hid, LANES), BF16)],
        compiler_params=params(("arbitrary",), 58 * 1024 * 1024),
        cost_estimate=pl.CostEstimate(
            flops=2 * rows * (days * hid + hid * hid + hid * LANES),
            bytes_accessed=2 * history.size + 4 * rows * LANES,
            transcendentals=0,
        ),
        name="bottom",
    )(history, w1, w2, w3)


def arrange_kernel(horizon, items, y_ref, out_ref):
    stores = y_ref.shape[0] // items
    lane = lax.broadcasted_iota(jnp.int32, (stores, LANES), 1)
    tiles = [None] * pl.cdiv(items * horizon, LANES)

    def add(t, v):
        tiles[t] = v if tiles[t] is None else tiles[t] + v

    for i in range(items):
        v = y_ref[pl.ds(i, stores, stride=items), :]
        t, off = divmod(i * horizon, LANES)
        if off:
            v = pltpu.roll(v, off, axis=1)
        if off + horizon > LANES:
            add(t, jnp.where(lane >= off, v, 0.0))
            add(t + 1, jnp.where(lane < off, v, 0.0))
        else:
            add(t, v)
    for t, v in enumerate(tiles):
        height = min(LANES, items * horizon - t * LANES)
        out_ref[t * LANES : t * LANES + height, :] = v.T[:height]


def arrange(y, items, horizon):
    rows = y.shape[0]
    return pl.pallas_call(
        functools.partial(arrange_kernel, horizon, items),
        in_specs=whole(1),
        out_specs=whole(1)[0],
        out_shape=jax.ShapeDtypeStruct((items * horizon, rows // items), F32),
        compiler_params=params(),
        cost_estimate=pl.CostEstimate(
            flops=rows * LANES * 4, bytes_accessed=rows * LANES * 4, transcendentals=0
        ),
        name="arrange",
    )(y)


def totals_kernel(chunk, s_ref, i_ref, w1_ref, w2_ref, w3_ref, col_ref, err_ref, item_ref, pay_ref, w3_wide):
    days = w1_ref.shape[0]
    widen(w3_ref, w3_wide)
    got = s_ref[0]
    for p in range(1, s_ref.shape[0]):
        got = got + s_ref[p]
    tiles = days // LANES
    x = jnp.concatenate([got[t * chunk : (t + 1) * chunk] for t in range(tiles)], axis=1)
    x = jnp.concatenate([x, i_ref[...]], axis=0)
    y = forecaster(x, w1_ref[...], w2_ref[...], w3_wide[...])
    fc = y[:chunk]
    fi = y[chunk:]
    item_ref[...] = fi
    q = chunk // 4
    err_ref[0:q, :] = pack_rows(fc) - got[tiles * chunk : tiles * chunk + q]
    err_ref[q : q + 1, :] = pltpu.roll(jnp.sum(fi, axis=0, keepdims=True), GROUP, axis=1)
    col = col_ref[...]
    sums = jnp.sum(fc, axis=0, keepdims=True) + pltpu.roll(
        jnp.sum(col, axis=0, keepdims=True), 2 * GROUP, axis=1
    )
    packed = pack_rows(col)
    n = packed.shape[0]
    for p in range(pay_ref.shape[0]):
        pay_ref[p, 0:n, :] = packed
        pay_ref[p, n : n + 1, :] = sums


def totals(store_parts, item_hist, w1, w2, w3, col, chunk, item_peers):
    items = item_hist.shape[0]
    return pl.pallas_call(
        functools.partial(totals_kernel, chunk),
        in_specs=whole(6),
        out_specs=whole(3),
        out_shape=[
            jax.ShapeDtypeStruct((8, LANES), F32),
            jax.ShapeDtypeStruct((items, LANES), F32),
            jax.ShapeDtypeStruct((item_peers, 8, LANES), F32),
        ],
        scratch_shapes=[pltpu.VMEM((w1.shape[1], LANES), BF16)],
        compiler_params=params(),
        name="totals",
    )(store_parts, item_hist, w1, w2, w3, col)


def middle_kernel(chunk, n, err_ref, got_ref, pay_ref):
    q = chunk // 4
    sums = err_ref[q : q + 1, :]
    for p in range(got_ref.shape[0]):
        sums = sums + got_ref[p, n : n + 1, :]
    err = err_ref[0:q, :]
    for p in range(pay_ref.shape[0]):
        pay_ref[p, 0:q, :] = err
        pay_ref[p, q : q + 1, :] = sums


def middle(err, got, chunk, items, peers):
    return pl.pallas_call(
        functools.partial(middle_kernel, chunk, items // 4),
        in_specs=whole(2),
        out_specs=whole(1)[0],
        out_shape=jax.ShapeDtypeStruct((peers, 8, LANES), F32),
        compiler_params=params(),
        name="middle",
    )(err, got)


def final_kernel(horizon, item_count, store_count, base_ref, item_ref, one_ref, two_ref, out_ref, sgap_ref, igap_ref, err_ref):
    width, stores = base_ref.shape
    items = width // horizon
    peers = two_ref.shape[0]
    valid1 = lax.broadcasted_iota(jnp.int32, (1, LANES), 1) < horizon

    def group(x, k):
        if k:
            x = pltpu.roll(x, LANES - k * GROUP, axis=1)
        return jnp.where(valid1, x, 0.0)

    n = items // 4
    colp = one_ref[0, 0:n, :]
    for p in range(1, one_ref.shape[0]):
        colp = colp + one_ref[p, 0:n, :]
    col = jnp.concatenate([group(colp, k) for k in range(4)], axis=0)
    item_err = item_ref[...] - col

    q = stores // peers // 4
    sums = two_ref[0, q : q + 1, :]
    for p in range(1, peers):
        sums = sums + two_ref[p, q : q + 1, :]
    total = group(sums, 2)
    err_s = group(sums, 0) - total
    err_i = group(sums, 1) - total
    for p in range(peers):
        for k in range(4):
            r = (p * 4 + k) * q
            err_ref[r : r + q, :] = group(two_ref[p, 0:q, :], k)
    store_err = err_ref[...].T[:horizon]

    denominator = 1.0 + item_count + store_count
    shift_s = (err_s * (1.0 + store_count) - store_count * err_i) / denominator
    shift_i = ((1.0 + item_count) * err_i - item_count * err_s) / denominator
    item_shift = (item_err - shift_s) / (1.0 + store_count)
    columns = jnp.concatenate(
        [item_shift, shift_i, jnp.zeros((LANES - items - 1, LANES), F32)], axis=0
    ).T[:horizon]
    store_shift = (store_err - columns[:, items : items + 1]) / (1.0 + item_count)

    a = jnp.concatenate([store_shift, store_shift], axis=0)
    b = jnp.concatenate([columns, pltpu.roll(columns, LANES - 1, axis=1)], axis=0)
    for j in range(items // 2):
        rows = slice(2 * j * horizon, (2 * j + 2) * horizon)
        out_ref[rows, :] = base_ref[rows, :] + a + b[:, 2 * j : 2 * j + 1]
    sgap_ref[...] = store_err * (1.0 / math.sqrt(item_count))
    igap_ref[...] = item_err[:, :horizon] * (1.0 / math.sqrt(store_count))


def final(base, item_fc, one, two, horizon, item_count, store_count):
    width, stores = base.shape
    items = width // horizon
    return pl.pallas_call(
        functools.partial(final_kernel, horizon, item_count, store_count),
        in_specs=whole(4),
        out_specs=whole(3),
        out_shape=[
            jax.ShapeDtypeStruct((width, stores), F32),
            jax.ShapeDtypeStruct((horizon, stores), F32),
            jax.ShapeDtypeStruct((items, horizon), F32),
        ],
        scratch_shapes=[pltpu.VMEM((stores, LANES), F32)],
        compiler_params=params(),
        name="final",
    )(base, item_fc, one, two)


def exchange(x, axis):
    return lax.all_to_all(x, axis, 0, 0, tiled=True)


def add_over(x, axis, flips):
    for flip in flips:
        pairs = [(i, i ^ flip) for i in range(lax.axis_size(axis))]
        x = x + lax.ppermute(x, axis, pairs)
    return x


def body(history, w1, w2, final_layer_matrix):
    stores, items, _ = history.shape
    horizon = final_layer_matrix.shape[1]
    n_store, n_dept = lax.axis_size("store"), lax.axis_size("dept")
    chunk = stores // n_dept
    w3 = final_layer_matrix.T

    pay, item_part, col, y = bottom(history, w1, w2, w3, n_dept, 64, 32)
    store_parts = exchange(pay, "dept")
    item_hist = add_over(item_part, "store", (1, 2, 4, 12))
    base = arrange(y, items, horizon)
    err, item_fc, pay_one = totals(store_parts, item_hist, w1, w2, w3, col, chunk, n_store)
    one = exchange(pay_one, "store")
    pay_two = middle(err, one, chunk, items, n_dept)
    two = exchange(pay_two, "dept")
    out, store_gap, item_gap = final(
        base, item_fc, one, two, horizon, float(items * n_dept), float(stores * n_store)
    )
    return out.T, store_gap, item_gap.T


def solution(mesh):
    return jax.shard_map(
        body,
        mesh=mesh,
        in_specs=(P("store", "dept", None), P(), P(), P()),
        out_specs=(P("store", "dept"), P(None, "store"), P(None, "dept")),
        check_vma=False,
    )
```

```python
import functools
import math

import jax
import jax.numpy as jnp
from jax import lax
from jax.experimental import pallas as pl
from jax.experimental.pallas import tpu as pltpu
from jax.sharding import PartitionSpec as P

F32 = jnp.float32
BF16 = jnp.bfloat16
LANES = 128
GROUP = 32
MIB = 1024 * 1024


def whole(n):
    return [pl.BlockSpec(memory_space=pltpu.VMEM)] * n


def params(mib):
    return pltpu.CompilerParams(vmem_limit_bytes=mib * MIB)


def stay(x):
    return pltpu.with_memory_space_constraint(x, pltpu.HBM)


def relu(x):
    return jnp.maximum(x.astype(BF16), 0)


def forecaster(x, w1, w2, w3):
    var = jnp.sum(x * x, axis=-1, keepdims=True) * (1.0 / x.shape[-1]) + 1e-05
    inv = lax.rsqrt(var)
    z = (x * inv).astype(BF16)
    a = relu(jnp.dot(z, w1, preferred_element_type=F32))
    b = relu(jnp.dot(a, w2, preferred_element_type=F32))
    return jnp.dot(b, w3, preferred_element_type=F32) * (var * inv)


def widen(w3_ref, w3_wide):
    horizon = w3_ref.shape[0]
    w3_wide[...] = jnp.zeros_like(w3_wide)
    w3_wide[:, :horizon] = w3_ref[...].astype(F32).T.astype(BF16)


def pack_rows(x):
    n = x.shape[0] // 4
    out = x[0:n]
    for k in range(1, 4):
        out = out + pltpu.roll(x[k * n : (k + 1) * n], k * GROUP, axis=1)
    return out


def bottom_kernel(chunk, part, h_ref, w1_ref, w2_ref, w3_ref, pay_ref, item_ref, col_ref, y_ref, w3_wide):
    block, items, days = h_ref.shape
    step = pl.program_id(0)

    @pl.when(step == 0)
    def _():
        widen(w3_ref, w3_wide)
        item_ref[...] = jnp.zeros_like(item_ref)
        col_ref[...] = jnp.zeros_like(col_ref)

    w1, w2, w3 = w1_ref[...], w2_ref[...], w3_wide[...]
    tiles = days // LANES
    for p in range(block // part):
        x = h_ref[p * part : (p + 1) * part].astype(F32)
        by_store = jnp.sum(x, axis=1)
        item_ref[...] += jnp.sum(x, axis=0)
        y = forecaster(x.reshape(part * items, days), w1, w2, w3)
        y_ref[p * part * items : (p + 1) * part * items, :] = y
        y = y.reshape(part, items, LANES)
        row = jnp.sum(y, axis=1)
        col_ref[...] += jnp.sum(y, axis=0)
        for q in range(part // chunk):
            peer = p * (part // chunk) + q
            for t in range(tiles):
                pay_ref[peer, t * chunk : (t + 1) * chunk, :] = by_store[
                    q * chunk : (q + 1) * chunk, t * LANES : (t + 1) * LANES
                ]
            pay_ref[peer, tiles * chunk : tiles * chunk + chunk // 4, :] = pack_rows(
                row[q * chunk : (q + 1) * chunk]
            )


def bottom(history, w1, w2, w3, peers, block, part):
    stores, items, days = history.shape
    hid = w1.shape[1]
    rows = stores * items
    chunk = stores // peers
    pay_rows = (days // LANES) * chunk + 8
    fixed = lambda shape: pl.BlockSpec(shape, lambda i: (0,) * len(shape))
    return pl.pallas_call(
        functools.partial(bottom_kernel, chunk, part),
        grid=(stores // block,),
        in_specs=[
            pl.BlockSpec((block, items, days), lambda i: (i, 0, 0)),
            fixed(w1.shape),
            fixed(w2.shape),
            fixed(w3.shape),
        ],
        out_specs=[
            pl.BlockSpec((block // chunk, pay_rows, LANES), lambda i: (i, 0, 0)),
            fixed((items, days)),
            fixed((items, LANES)),
            pl.BlockSpec((block * items, LANES), lambda i: (i, 0)),
        ],
        out_shape=[
            jax.ShapeDtypeStruct((peers, pay_rows, LANES), F32),
            jax.ShapeDtypeStruct((items, days), F32),
            jax.ShapeDtypeStruct((items, LANES), F32),
            pltpu.HBM((rows, LANES), F32),
        ],
        scratch_shapes=[pltpu.VMEM((hid, LANES), BF16)],
        compiler_params=params(24),
        cost_estimate=pl.CostEstimate(
            flops=2 * rows * (days * hid + hid * hid + hid * LANES),
            bytes_accessed=2 * history.size + 4 * rows * LANES,
            transcendentals=0,
        ),
        name="bottom",
    )(stay(history), stay(w1), stay(w2), stay(w3))


def arrange_kernel(horizon, items, y_ref, out_ref):
    stores = y_ref.shape[0] // items
    lane = lax.broadcasted_iota(jnp.int32, (stores, LANES), 1)
    tiles = [None] * pl.cdiv(items * horizon, LANES)

    def add(t, v):
        tiles[t] = v if tiles[t] is None else tiles[t] + v

    for i in range(items):
        v = y_ref[pl.ds(i, stores, stride=items), :]
        t, off = divmod(i * horizon, LANES)
        if off:
            v = pltpu.roll(v, off, axis=1)
        if off + horizon > LANES:
            add(t, jnp.where(lane >= off, v, 0.0))
            add(t + 1, jnp.where(lane < off, v, 0.0))
        else:
            add(t, v)
    for t, v in enumerate(tiles):
        height = min(LANES, items * horizon - t * LANES)
        out_ref[t * LANES : t * LANES + height, :] = v.T[:height]


def arrange(y, items, horizon):
    rows = y.shape[0]
    return pl.pallas_call(
        functools.partial(arrange_kernel, horizon, items),
        in_specs=whole(1),
        out_specs=whole(1)[0],
        out_shape=jax.ShapeDtypeStruct((items * horizon, rows // items), F32),
        compiler_params=params(12),
        cost_estimate=pl.CostEstimate(
            flops=rows * LANES * 4, bytes_accessed=rows * LANES * 4, transcendentals=0
        ),
        name="arrange",
    )(y)


def totals_kernel(chunk, s_ref, i_ref, w1_ref, w2_ref, w3_ref, col_ref, err_ref, item_ref, pay_ref, w3_wide):
    days = w1_ref.shape[0]
    widen(w3_ref, w3_wide)
    got = s_ref[0]
    for p in range(1, s_ref.shape[0]):
        got = got + s_ref[p]
    tiles = days // LANES
    x = jnp.concatenate([got[t * chunk : (t + 1) * chunk] for t in range(tiles)], axis=1)
    x = jnp.concatenate([x, i_ref[...]], axis=0)
    y = forecaster(x, w1_ref[...], w2_ref[...], w3_wide[...])
    fc = y[:chunk]
    fi = y[chunk:]
    item_ref[...] = fi
    q = chunk // 4
    err_ref[0:q, :] = pack_rows(fc) - got[tiles * chunk : tiles * chunk + q]
    err_ref[q : q + 1, :] = pltpu.roll(jnp.sum(fi, axis=0, keepdims=True), GROUP, axis=1)
    col = col_ref[...]
    sums = jnp.sum(fc, axis=0, keepdims=True) + pltpu.roll(
        jnp.sum(col, axis=0, keepdims=True), 2 * GROUP, axis=1
    )
    packed = pack_rows(col)
    n = packed.shape[0]
    for p in range(pay_ref.shape[0]):
        pay_ref[p, 0:n, :] = packed
        pay_ref[p, n : n + 1, :] = sums


def totals(store_parts, item_hist, w1, w2, w3, col, chunk, item_peers):
    items = item_hist.shape[0]
    return pl.pallas_call(
        functools.partial(totals_kernel, chunk),
        in_specs=whole(6),
        out_specs=whole(3),
        out_shape=[
            jax.ShapeDtypeStruct((8, LANES), F32),
            jax.ShapeDtypeStruct((items, LANES), F32),
            jax.ShapeDtypeStruct((item_peers, 8, LANES), F32),
        ],
        scratch_shapes=[pltpu.VMEM((w1.shape[1], LANES), BF16)],
        compiler_params=params(8),
        name="totals",
    )(store_parts, item_hist, w1, w2, w3, col)


def middle_kernel(chunk, n, err_ref, got_ref, pay_ref):
    q = chunk // 4
    sums = err_ref[q : q + 1, :]
    for p in range(got_ref.shape[0]):
        sums = sums + got_ref[p, n : n + 1, :]
    err = err_ref[0:q, :]
    for p in range(pay_ref.shape[0]):
        pay_ref[p, 0:q, :] = err
        pay_ref[p, q : q + 1, :] = sums


def middle(err, got, chunk, items, peers):
    return pl.pallas_call(
        functools.partial(middle_kernel, chunk, items // 4),
        in_specs=whole(2),
        out_specs=whole(1)[0],
        out_shape=jax.ShapeDtypeStruct((peers, 8, LANES), F32),
        compiler_params=params(2),
        name="middle",
    )(err, got)


def final_kernel(horizon, item_count, store_count, base_ref, item_ref, one_ref, two_ref, out_ref, sgap_ref, igap_ref, err_ref):
    width, stores = base_ref.shape
    items = width // horizon
    peers = two_ref.shape[0]
    valid1 = lax.broadcasted_iota(jnp.int32, (1, LANES), 1) < horizon

    def group(x, k):
        if k:
            x = pltpu.roll(x, LANES - k * GROUP, axis=1)
        return jnp.where(valid1, x, 0.0)

    n = items // 4
    colp = one_ref[0, 0:n, :]
    for p in range(1, one_ref.shape[0]):
        colp = colp + one_ref[p, 0:n, :]
    col = jnp.concatenate([group(colp, k) for k in range(4)], axis=0)
    item_err = item_ref[...] - col

    q = stores // peers // 4
    sums = two_ref[0, q : q + 1, :]
    for p in range(1, peers):
        sums = sums + two_ref[p, q : q + 1, :]
    total = group(sums, 2)
    err_s = group(sums, 0) - total
    err_i = group(sums, 1) - total
    for p in range(peers):
        for k in range(4):
            r = (p * 4 + k) * q
            err_ref[r : r + q, :] = group(two_ref[p, 0:q, :], k)
    store_err = err_ref[...].T[:horizon]

    denominator = 1.0 + item_count + store_count
    shift_s = (err_s * (1.0 + store_count) - store_count * err_i) / denominator
    shift_i = ((1.0 + item_count) * err_i - item_count * err_s) / denominator
    item_shift = (item_err - shift_s) / (1.0 + store_count)
    columns = jnp.concatenate(
        [item_shift, shift_i, jnp.zeros((LANES - items - 1, LANES), F32)], axis=0
    ).T[:horizon]
    store_shift = (store_err - columns[:, items : items + 1]) / (1.0 + item_count)

    a = jnp.concatenate([store_shift, store_shift], axis=0)
    b = jnp.concatenate([columns, pltpu.roll(columns, LANES - 1, axis=1)], axis=0)
    for j in range(items // 2):
        rows = slice(2 * j * horizon, (2 * j + 2) * horizon)
        out_ref[rows, :] = base_ref[rows, :] + a + b[:, 2 * j : 2 * j + 1]
    sgap_ref[...] = store_err * (1.0 / math.sqrt(item_count))
    igap_ref[...] = item_err[:, :horizon] * (1.0 / math.sqrt(store_count))


def final(base, item_fc, one, two, horizon, item_count, store_count):
    width, stores = base.shape
    items = width // horizon
    return pl.pallas_call(
        functools.partial(final_kernel, horizon, item_count, store_count),
        in_specs=whole(4),
        out_specs=whole(3),
        out_shape=[
            jax.ShapeDtypeStruct((width, stores), F32),
            jax.ShapeDtypeStruct((horizon, stores), F32),
            jax.ShapeDtypeStruct((items, horizon), F32),
        ],
        scratch_shapes=[pltpu.VMEM((stores, LANES), F32)],
        compiler_params=params(6),
        name="final",
    )(base, item_fc, one, two)


def exchange(x, axis):
    return lax.all_to_all(x, axis, 0, 0, tiled=True)


def partner(x, axis, flip):
    return lax.ppermute(x, axis, [(i, i ^ flip) for i in range(lax.axis_size(axis))])


def add_over_stores(x):
    x = x + partner(x, "store", 1)
    x = x + partner(x, "store", 2)
    near, far, across = (partner(x, "store", flip) for flip in (4, 12, 8))
    return (x + across) + (near + far)


def body(history, w1, w2, final_layer_matrix):
    stores, items, _ = history.shape
    horizon = final_layer_matrix.shape[1]
    n_store, n_dept = lax.axis_size("store"), lax.axis_size("dept")
    chunk = stores // n_dept
    w3 = final_layer_matrix.T

    pay, item_part, col, y = bottom(history, w1, w2, w3, n_dept, 64, 32)
    store_parts = exchange(pay, "dept")
    item_hist = add_over_stores(item_part)
    base, item_hist = lax.optimization_barrier((arrange(stay(y), items, horizon), item_hist))
    err, item_fc, pay_one = totals(store_parts, item_hist, w1, w2, w3, col, chunk, n_store)
    one = exchange(pay_one, "store")
    pay_two = middle(err, one, chunk, items, n_dept)
    two = exchange(pay_two, "dept")
    out, store_gap, item_gap = final(
        base, item_fc, one, two, horizon, float(items * n_dept), float(stores * n_store)
    )
    return out.T, store_gap, item_gap.T


def solution(mesh):
    return jax.shard_map(
        body,
        mesh=mesh,
        in_specs=(P("store", "dept", None), P(), P(), P()),
        out_specs=(P("store", "dept"), P(None, "store"), P(None, "dept")),
        check_vma=False,
    )
```

```python
import functools
import math

import jax
import jax.numpy as jnp
from jax import lax
from jax.experimental import pallas as pl
from jax.experimental.pallas import tpu as pltpu
from jax.sharding import PartitionSpec as P

F32 = jnp.float32
BF16 = jnp.bfloat16
LANES = 128
GROUP = 32
MIB = 1024 * 1024


def whole(n):
    return [pl.BlockSpec(memory_space=pltpu.VMEM)] * n


def params(mib):
    return pltpu.CompilerParams(vmem_limit_bytes=mib * MIB)


def stay(x):
    return pltpu.with_memory_space_constraint(x, pltpu.HBM)


def relu(x):
    return jnp.maximum(x.astype(BF16), 0)


def forecaster(x, w1, w2, w3):
    var = jnp.sum(x * x, axis=-1, keepdims=True) * (1.0 / x.shape[-1]) + 1e-05
    inv = lax.rsqrt(var)
    z = (x * inv).astype(BF16)
    a = relu(jnp.dot(z, w1, preferred_element_type=F32))
    b = relu(jnp.dot(a, w2, preferred_element_type=F32))
    return jnp.dot(b, w3, preferred_element_type=F32) * (var * inv)


def widen(w3_ref, w3_wide):
    horizon = w3_ref.shape[0]
    w3_wide[...] = jnp.zeros_like(w3_wide)
    w3_wide[:, :horizon] = w3_ref[...].astype(F32).T.astype(BF16)


def pack_rows(x):
    n = x.shape[0] // 4
    out = x[0:n]
    for k in range(1, 4):
        out = out + pltpu.roll(x[k * n : (k + 1) * n], k * GROUP, axis=1)
    return out


def early_kernel(chunk, part, late, h_ref, w1_ref, w2_ref, w3_ref, pay_ref, item_ref, col_ref, y_ref, w3_wide):
    block, items, days = h_ref.shape
    step = pl.program_id(0)
    tiles = days // LANES

    @pl.when(step == 0)
    def _():
        widen(w3_ref, w3_wide)
        item_ref[...] = jnp.zeros_like(item_ref)
        col_ref[...] = jnp.zeros_like(col_ref)

    def sums(p):
        x = h_ref[p * part : (p + 1) * part].astype(F32)
        by_store = jnp.sum(x, axis=1)
        item_ref[...] += jnp.sum(x, axis=0)
        for q in range(part // chunk):
            for t in range(tiles):
                pay_ref[p * (part // chunk) + q, t * chunk : (t + 1) * chunk, :] = by_store[
                    q * chunk : (q + 1) * chunk, t * LANES : (t + 1) * LANES
                ]
        return x

    @pl.when(step < late)
    def _():
        for p in range(block // part):
            sums(p)
        pay_ref[:, tiles * chunk :, :] = jnp.zeros((block // chunk, 8, LANES), F32)

    @pl.when(step >= late)
    def _():
        w1, w2, w3 = w1_ref[...], w2_ref[...], w3_wide[...]
        for p in range(block // part):
            x = sums(p)
            y = forecaster(x.reshape(part * items, days), w1, w2, w3)
            y_ref[p * part * items : (p + 1) * part * items, :] = y
            y = y.reshape(part, items, LANES)
            row = jnp.sum(y, axis=1)
            col_ref[...] += jnp.sum(y, axis=0)
            for q in range(part // chunk):
                pay_ref[p * (part // chunk) + q, tiles * chunk : tiles * chunk + chunk // 4, :] = (
                    pack_rows(row[q * chunk : (q + 1) * chunk])
                )


def early(history, w1, w2, w3, peers, block, part, late):
    stores, items, days = history.shape
    hid = w1.shape[1]
    blocks = stores // block
    rows = (blocks - late) * block * items
    chunk = stores // peers
    pay_rows = (days // LANES) * chunk + 8
    fixed = lambda shape: pl.BlockSpec(shape, lambda i: (0,) * len(shape))
    turn = lambda i: lax.rem(i + blocks - late, blocks)
    return pl.pallas_call(
        functools.partial(early_kernel, chunk, part, late),
        grid=(blocks,),
        in_specs=[
            pl.BlockSpec((block, items, days), lambda i: (turn(i), 0, 0)),
            fixed(w1.shape),
            fixed(w2.shape),
            fixed(w3.shape),
        ],
        out_specs=[
            pl.BlockSpec((block // chunk, pay_rows, LANES), lambda i: (turn(i), 0, 0)),
            fixed((items, days)),
            fixed((items, LANES)),
            pl.BlockSpec((block * items, LANES), lambda i: (jnp.maximum(i - late, 0), 0)),
        ],
        out_shape=[
            jax.ShapeDtypeStruct((peers, pay_rows, LANES), F32),
            jax.ShapeDtypeStruct((items, days), F32),
            jax.ShapeDtypeStruct((items, LANES), F32),
            pltpu.HBM((rows, LANES), F32),
        ],
        scratch_shapes=[pltpu.VMEM((hid, LANES), BF16)],
        compiler_params=params(24),
        cost_estimate=pl.CostEstimate(
            flops=2 * rows * (days * hid + hid * hid + hid * LANES),
            bytes_accessed=2 * history.size + 4 * rows * LANES,
            transcendentals=0,
        ),
        name="early",
    )(stay(history), stay(w1), stay(w2), stay(w3))


def late_kernel(part, h_ref, w1_ref, w2_ref, w3_ref, row_ref, col_ref, y_ref, w3_wide):
    block, items, days = h_ref.shape

    @pl.when(pl.program_id(0) == 0)
    def _():
        widen(w3_ref, w3_wide)
        col_ref[...] = jnp.zeros_like(col_ref)

    w1, w2, w3 = w1_ref[...], w2_ref[...], w3_wide[...]
    rows = []
    for p in range(block // part):
        x = h_ref[p * part : (p + 1) * part].astype(F32).reshape(part * items, days)
        y = forecaster(x, w1, w2, w3)
        y_ref[p * part * items : (p + 1) * part * items, :] = y
        y = y.reshape(part, items, LANES)
        rows.append(jnp.sum(y, axis=1))
        col_ref[...] += jnp.sum(y, axis=0)
    row_ref[0] = pack_rows(jnp.concatenate(rows, axis=0))


def late_forecasts(history, w1, w2, w3, block, part, late):
    stores, items, days = history.shape
    hid = w1.shape[1]
    rows = late * block * items
    skip = stores // block - late
    fixed = lambda shape: pl.BlockSpec(shape, lambda i: (0,) * len(shape))
    return pl.pallas_call(
        functools.partial(late_kernel, part),
        grid=(late,),
        in_specs=[
            pl.BlockSpec((block, items, days), lambda i: (i + skip, 0, 0)),
            fixed(w1.shape),
            fixed(w2.shape),
            fixed(w3.shape),
        ],
        out_specs=[
            pl.BlockSpec((1, block // 4, LANES), lambda i: (i, 0, 0)),
            fixed((items, LANES)),
            pl.BlockSpec((block * items, LANES), lambda i: (i, 0)),
        ],
        out_shape=[
            jax.ShapeDtypeStruct((late, block // 4, LANES), F32),
            jax.ShapeDtypeStruct((items, LANES), F32),
            pltpu.HBM((rows, LANES), F32),
        ],
        scratch_shapes=[pltpu.VMEM((hid, LANES), BF16)],
        compiler_params=params(24),
        cost_estimate=pl.CostEstimate(
            flops=2 * rows * (days * hid + hid * hid + hid * LANES),
            bytes_accessed=2 * rows * days + 4 * rows * LANES,
            transcendentals=0,
        ),
        name="late",
    )(stay(history), w1, w2, w3)


def arrange_kernel(horizon, items, early_ref, late_ref, out_ref):
    first = 0
    for y_ref in (early_ref, late_ref):
        stores = y_ref.shape[0] // items
        lane = lax.broadcasted_iota(jnp.int32, (stores, LANES), 1)
        tiles = [None] * pl.cdiv(items * horizon, LANES)

        def add(t, v):
            tiles[t] = v if tiles[t] is None else tiles[t] + v

        for i in range(items):
            v = y_ref[pl.ds(i, stores, stride=items), :]
            t, off = divmod(i * horizon, LANES)
            if off:
                v = pltpu.roll(v, off, axis=1)
            if off + horizon > LANES:
                add(t, jnp.where(lane >= off, v, 0.0))
                add(t + 1, jnp.where(lane < off, v, 0.0))
            else:
                add(t, v)
        for t, v in enumerate(tiles):
            height = min(LANES, items * horizon - t * LANES)
            out_ref[t * LANES : t * LANES + height, first : first + stores] = v.T[:height]
        first += stores


def arrange(early_y, late_y, items, horizon):
    rows = early_y.shape[0] + late_y.shape[0]
    return pl.pallas_call(
        functools.partial(arrange_kernel, horizon, items),
        in_specs=whole(2),
        out_specs=whole(1)[0],
        out_shape=jax.ShapeDtypeStruct((items * horizon, rows // items), F32),
        compiler_params=params(12),
        cost_estimate=pl.CostEstimate(
            flops=rows * LANES * 4, bytes_accessed=rows * LANES * 4, transcendentals=0
        ),
        name="arrange",
    )(stay(early_y), stay(late_y))


def totals_kernel(chunk, s_ref, i_ref, w1_ref, w2_ref, w3_ref, col_ref, col_late_ref, err_ref, item_ref, pay_ref, w3_wide):
    days = w1_ref.shape[0]
    widen(w3_ref, w3_wide)
    got = s_ref[0]
    for p in range(1, s_ref.shape[0]):
        got = got + s_ref[p]
    tiles = days // LANES
    x = jnp.concatenate([got[t * chunk : (t + 1) * chunk] for t in range(tiles)], axis=1)
    x = jnp.concatenate([x, i_ref[...]], axis=0)
    y = forecaster(x, w1_ref[...], w2_ref[...], w3_wide[...])
    fc = y[:chunk]
    fi = y[chunk:]
    item_ref[...] = fi
    q = chunk // 4
    err_ref[0:q, :] = pack_rows(fc) - got[tiles * chunk : tiles * chunk + q]
    err_ref[q : q + 1, :] = pltpu.roll(jnp.sum(fi, axis=0, keepdims=True), GROUP, axis=1)
    col = col_ref[...] + col_late_ref[...]
    sums = jnp.sum(fc, axis=0, keepdims=True) + pltpu.roll(
        jnp.sum(col, axis=0, keepdims=True), 2 * GROUP, axis=1
    )
    packed = pack_rows(col)
    n = packed.shape[0]
    for p in range(pay_ref.shape[0]):
        pay_ref[p, 0:n, :] = packed
        pay_ref[p, n : n + 1, :] = sums


def totals(store_parts, item_hist, w1, w2, w3, col, col_late, chunk, item_peers):
    items = item_hist.shape[0]
    return pl.pallas_call(
        functools.partial(totals_kernel, chunk),
        in_specs=whole(7),
        out_specs=whole(3),
        out_shape=[
            jax.ShapeDtypeStruct((8, LANES), F32),
            jax.ShapeDtypeStruct((items, LANES), F32),
            jax.ShapeDtypeStruct((item_peers, 8, LANES), F32),
        ],
        scratch_shapes=[pltpu.VMEM((w1.shape[1], LANES), BF16)],
        compiler_params=params(8),
        name="totals",
    )(store_parts, item_hist, w1, w2, w3, col, col_late)


def middle_kernel(chunk, n, err_ref, keep_ref, came_ref, got_ref, pay_ref):
    q = chunk // 4
    sums = err_ref[q : q + 1, :]
    for p in range(got_ref.shape[0]):
        sums = sums + got_ref[p, n : n + 1, :]
    err = err_ref[0:q, :]
    late = keep_ref[...] + came_ref[...]
    for p in range(pay_ref.shape[0]):
        pay_ref[p, 0:q, :] = err
        pay_ref[p, q : q + 1, :] = sums
        pay_ref[p, 8:, :] = late


def middle(err, keep, came, got, chunk, items, peers):
    return pl.pallas_call(
        functools.partial(middle_kernel, chunk, items // 4),
        in_specs=whole(4),
        out_specs=whole(1)[0],
        out_shape=jax.ShapeDtypeStruct((peers, 8 + keep.shape[0], LANES), F32),
        compiler_params=params(2),
        name="middle",
    )(err, keep, came, got)


def final_kernel(horizon, item_count, store_count, base_ref, item_ref, one_ref, two_ref, out_ref, sgap_ref, igap_ref, err_ref):
    width, stores = base_ref.shape
    items = width // horizon
    peers = two_ref.shape[0]
    valid1 = lax.broadcasted_iota(jnp.int32, (1, LANES), 1) < horizon

    def group(x, k):
        if k:
            x = pltpu.roll(x, LANES - k * GROUP, axis=1)
        return jnp.where(valid1, x, 0.0)

    n = items // 4
    colp = one_ref[0, 0:n, :]
    for p in range(1, one_ref.shape[0]):
        colp = colp + one_ref[p, 0:n, :]
    col = jnp.concatenate([group(colp, k) for k in range(4)], axis=0)
    item_err = item_ref[...] - col

    q = stores // peers // 4
    sums = two_ref[0, q : q + 1, :]
    for p in range(1, peers):
        sums = sums + two_ref[p, q : q + 1, :]
    total = group(sums, 2)
    err_s = group(sums, 0) - total
    err_i = group(sums, 1) - total
    for p in range(peers):
        for k in range(4):
            r = (p * 4 + k) * q
            err_ref[r : r + q, :] = group(two_ref[p, 0:q, :], k)
    n_late = two_ref.shape[1] - 8
    for odd in range(2):
        row = two_ref[odd, 8:, :]
        for p in range(odd + 2, peers, 2):
            row = row + two_ref[p, 8:, :]
        for k in range(4):
            r = stores - (2 - odd) * 4 * n_late + k * n_late
            err_ref[r : r + n_late, :] -= group(row, k)
    store_err = err_ref[...].T[:horizon]

    denominator = 1.0 + item_count + store_count
    shift_s = (err_s * (1.0 + store_count) - store_count * err_i) / denominator
    shift_i = ((1.0 + item_count) * err_i - item_count * err_s) / denominator
    item_shift = (item_err - shift_s) / (1.0 + store_count)
    columns = jnp.concatenate(
        [item_shift, shift_i, jnp.zeros((LANES - items - 1, LANES), F32)], axis=0
    ).T[:horizon]
    store_shift = (store_err - columns[:, items : items + 1]) / (1.0 + item_count)

    a = jnp.concatenate([store_shift, store_shift], axis=0)
    b = jnp.concatenate([columns, pltpu.roll(columns, LANES - 1, axis=1)], axis=0)
    for j in range(items // 2):
        rows = slice(2 * j * horizon, (2 * j + 2) * horizon)
        out_ref[rows, :] = base_ref[rows, :] + a + b[:, 2 * j : 2 * j + 1]
    sgap_ref[...] = store_err * (1.0 / math.sqrt(item_count))
    igap_ref[...] = item_err[:, :horizon] * (1.0 / math.sqrt(store_count))


def final(base, item_fc, one, two, horizon, item_count, store_count):
    width, stores = base.shape
    items = width // horizon
    return pl.pallas_call(
        functools.partial(final_kernel, horizon, item_count, store_count),
        in_specs=whole(4),
        out_specs=whole(3),
        out_shape=[
            jax.ShapeDtypeStruct((width, stores), F32),
            jax.ShapeDtypeStruct((horizon, stores), F32),
            jax.ShapeDtypeStruct((items, horizon), F32),
        ],
        scratch_shapes=[pltpu.VMEM((stores, LANES), F32)],
        compiler_params=params(6),
        name="final",
    )(base, item_fc, one, two)


def exchange(x, axis):
    return lax.all_to_all(x, axis, 0, 0, tiled=True)


def partner(x, axis, flip):
    return lax.ppermute(x, axis, [(i, i ^ flip) for i in range(lax.axis_size(axis))])


def add_over_x(x):
    x = x + partner(x, "store", 1)
    return x + partner(x, "store", 2)


def add_over_y(x):
    near, far, across = (partner(x, "store", flip) for flip in (4, 12, 8))
    return (x + across) + (near + far)


def body(history, w1, w2, final_layer_matrix):
    stores, items, _ = history.shape
    horizon = final_layer_matrix.shape[1]
    n_store, n_dept = lax.axis_size("store"), lax.axis_size("dept")
    chunk = stores // n_dept
    w3 = final_layer_matrix.T

    block, part, late = stores // 4, stores // 8, 2
    pay, item_part, col, y = early(history, w1, w2, w3, n_dept, block, part, late)
    store_parts = exchange(pay, "dept")
    item_hist = add_over_x(item_part)
    late_rows, late_col, late_y = late_forecasts(history, w1, w2, w3, block, part, late)
    late_rows, late_y, item_hist = lax.optimization_barrier((late_rows, late_y, item_hist))
    item_hist = add_over_y(item_hist)
    odd = lax.rem(lax.axis_index("dept"), 2) == 1
    keep = jnp.where(odd, late_rows[1], late_rows[0])
    came = partner(jnp.where(odd, late_rows[0], late_rows[1]), "dept", 1)
    base = arrange(y, late_y, items, horizon)
    base, item_hist, came = lax.optimization_barrier((base, item_hist, came))
    err, item_fc, pay_one = totals(
        store_parts, item_hist, w1, w2, w3, col, late_col, chunk, n_store
    )
    one = exchange(pay_one, "store")
    pay_two = middle(err, keep, came, one, chunk, items, n_dept)
    two = exchange(pay_two, "dept")
    out, store_gap, item_gap = final(
        base, item_fc, one, two, horizon, float(items * n_dept), float(stores * n_store)
    )
    return out.T, store_gap, item_gap.T


def solution(mesh):
    return jax.shard_map(
        body,
        mesh=mesh,
        in_specs=(P("store", "dept", None), P(), P(), P()),
        out_specs=(P("store", "dept"), P(None, "store"), P(None, "dept")),
        check_vma=False,
    )
```

```python
import functools
import math

import jax
import jax.numpy as jnp
from jax import lax
from jax.experimental import pallas as pl
from jax.experimental.pallas import tpu as pltpu
from jax.sharding import PartitionSpec as P

F32 = jnp.float32
BF16 = jnp.bfloat16
LANES = 128
GROUP = 32
MIB = 1024 * 1024


def whole(n):
    return [pl.BlockSpec(memory_space=pltpu.VMEM)] * n


def params(mib):
    return pltpu.CompilerParams(vmem_limit_bytes=mib * MIB)


def stay(x):
    return pltpu.with_memory_space_constraint(x, pltpu.HBM)


def relu(x):
    return jnp.maximum(x.astype(BF16), 0)


def forecaster(x, w1, w2, w3):
    var = jnp.sum(x * x, axis=-1, keepdims=True) * (1.0 / x.shape[-1]) + 1e-05
    inv = lax.rsqrt(var)
    z = (x * inv).astype(BF16)
    a = relu(jnp.dot(z, w1, preferred_element_type=F32))
    b = relu(jnp.dot(a, w2, preferred_element_type=F32))
    return jnp.dot(b, w3, preferred_element_type=F32) * (var * inv)


def sum_items(x):
    stores, items, width = x.shape
    x = x.reshape(stores, items // 8, 8, width)
    total = x[:, 0]
    for k in range(1, items // 8):
        total = total + x[:, k]
    v = total.reshape(stores // 8, 8, 8, width)
    row = lax.broadcasted_iota(jnp.int32, (1, 1, 8, width), 2)
    for bit in (4, 2, 1):
        low = lax.rem(lax.div(row, bit), 2) == 0
        a, b = v[:, :bit], v[:, bit:]
        there = jnp.where(low, b, a)
        up = pltpu.roll(there, bit, axis=2)
        if bit < 4:
            up = jnp.where(low, pltpu.roll(there, 8 - bit, axis=2), up)
        v = jnp.where(low, a, b) + up
    return v.reshape(stores, width)


def widen(w3_ref, w3_wide):
    horizon = w3_ref.shape[0]
    w3_wide[...] = jnp.zeros_like(w3_wide)
    w3_wide[:, :horizon] = w3_ref[...].astype(F32).T.astype(BF16)


def pack_rows(x):
    n = x.shape[0] // 4
    out = x[0:n]
    for k in range(1, 4):
        out = out + pltpu.roll(x[k * n : (k + 1) * n], k * GROUP, axis=1)
    return out


def bottom_kernel(chunk, part, h_ref, w1_ref, w2_ref, w3_ref, pay_ref, item_ref, col_ref, y_ref, w3_wide):
    block, items, days = h_ref.shape
    step = pl.program_id(0)

    @pl.when(step == 0)
    def _():
        widen(w3_ref, w3_wide)
        item_ref[...] = jnp.zeros_like(item_ref)
        col_ref[...] = jnp.zeros_like(col_ref)
        y_ref[...] = jnp.zeros_like(y_ref)

    w1, w2, w3 = w1_ref[...], w2_ref[...], w3_wide[...]
    tiles = days // LANES
    for p in range(block // part):
        x = h_ref[p * part : (p + 1) * part].astype(F32)
        by_store = sum_items(x)
        item_ref[...] += jnp.sum(x, axis=0)
        y = forecaster(x.reshape(part * items, days), w1, w2, w3)
        y_ref[p * part * items : (p + 1) * part * items, :] += pltpu.roll(y, step * GROUP, axis=1)
        y = y.reshape(part, items, LANES)
        row = sum_items(y)
        col_ref[...] += jnp.sum(y, axis=0)
        for q in range(part // chunk):
            peer = p * (part // chunk) + q
            for t in range(tiles):
                pay_ref[peer, t * chunk : (t + 1) * chunk, :] = by_store[
                    q * chunk : (q + 1) * chunk, t * LANES : (t + 1) * LANES
                ]
            pay_ref[peer, tiles * chunk : tiles * chunk + chunk // 4, :] = pack_rows(
                row[q * chunk : (q + 1) * chunk]
            )


def bottom(history, w1, w2, w3, peers, block, part):
    stores, items, days = history.shape
    hid = w1.shape[1]
    rows = stores * items
    chunk = stores // peers
    pay_rows = (days // LANES) * chunk + 8
    fixed = lambda shape: pl.BlockSpec(shape, lambda i: (0,) * len(shape))
    return pl.pallas_call(
        functools.partial(bottom_kernel, chunk, part),
        grid=(stores // block,),
        in_specs=[
            pl.BlockSpec((block, items, days), lambda i: (i, 0, 0)),
            fixed(w1.shape),
            fixed(w2.shape),
            fixed(w3.shape),
        ],
        out_specs=[
            pl.BlockSpec((block // chunk, pay_rows, LANES), lambda i: (i, 0, 0)),
            fixed((items, days)),
            fixed((items, LANES)),
            fixed((block * items, LANES)),
        ],
        out_shape=[
            jax.ShapeDtypeStruct((peers, pay_rows, LANES), F32),
            jax.ShapeDtypeStruct((items, days), F32),
            jax.ShapeDtypeStruct((items, LANES), F32),
            jax.ShapeDtypeStruct((block * items, LANES), F32),
        ],
        scratch_shapes=[pltpu.VMEM((hid, LANES), BF16)],
        compiler_params=params(24),
        cost_estimate=pl.CostEstimate(
            flops=2 * rows * (days * hid + hid * hid + hid * LANES),
            bytes_accessed=2 * history.size,
            transcendentals=0,
        ),
        name="bottom",
    )(stay(history), stay(w1), stay(w2), stay(w3))


def arrange_kernel(horizon, items, y_ref, out_ref):
    block = y_ref.shape[0] // items
    for i in range(items):
        v = y_ref[pl.ds(i, block, stride=items), :].T
        blocks = [v[k * GROUP : k * GROUP + horizon] for k in range(LANES // GROUP)]
        out_ref[i * horizon : (i + 1) * horizon, :] = jnp.concatenate(blocks, axis=1)


def arrange(y, items, horizon):
    rows = y.shape[0]
    stores = rows // items * (LANES // GROUP)
    return pl.pallas_call(
        functools.partial(arrange_kernel, horizon, items),
        in_specs=whole(1),
        out_specs=whole(1)[0],
        out_shape=jax.ShapeDtypeStruct((items * horizon, stores), F32),
        compiler_params=params(12),
        cost_estimate=pl.CostEstimate(
            flops=16 * rows * LANES, bytes_accessed=12 * rows * LANES, transcendentals=0
        ),
        name="arrange",
    )(y)


def totals_kernel(chunk, s_ref, i_ref, w1_ref, w2_ref, w3_ref, col_ref, err_ref, item_ref, pay_ref, w3_wide):
    days = w1_ref.shape[0]
    widen(w3_ref, w3_wide)
    got = s_ref[0]
    for p in range(1, s_ref.shape[0]):
        got = got + s_ref[p]
    tiles = days // LANES
    x = jnp.concatenate([got[t * chunk : (t + 1) * chunk] for t in range(tiles)], axis=1)
    x = jnp.concatenate([x, i_ref[...]], axis=0)
    y = forecaster(x, w1_ref[...], w2_ref[...], w3_wide[...])
    fc = y[:chunk]
    fi = y[chunk:]
    item_ref[...] = fi
    q = chunk // 4
    err_ref[0:q, :] = pack_rows(fc) - got[tiles * chunk : tiles * chunk + q]
    err_ref[q : q + 1, :] = pltpu.roll(jnp.sum(fi, axis=0, keepdims=True), GROUP, axis=1)
    col = col_ref[...]
    sums = jnp.sum(fc, axis=0, keepdims=True) + pltpu.roll(
        jnp.sum(col, axis=0, keepdims=True), 2 * GROUP, axis=1
    )
    packed = pack_rows(col)
    n = packed.shape[0]
    for p in range(pay_ref.shape[0]):
        pay_ref[p, 0:n, :] = packed
        pay_ref[p, n : n + 1, :] = sums


def totals(store_parts, item_hist, w1, w2, w3, col, chunk, item_peers):
    items = item_hist.shape[0]
    return pl.pallas_call(
        functools.partial(totals_kernel, chunk),
        in_specs=whole(6),
        out_specs=whole(3),
        out_shape=[
            jax.ShapeDtypeStruct((8, LANES), F32),
            jax.ShapeDtypeStruct((items, LANES), F32),
            jax.ShapeDtypeStruct((item_peers, 8, LANES), F32),
        ],
        scratch_shapes=[pltpu.VMEM((w1.shape[1], LANES), BF16)],
        compiler_params=params(8),
        name="totals",
    )(store_parts, item_hist, w1, w2, w3, col)


def middle_kernel(chunk, n, err_ref, got_ref, pay_ref):
    q = chunk // 4
    sums = err_ref[q : q + 1, :]
    for p in range(got_ref.shape[0]):
        sums = sums + got_ref[p, n : n + 1, :]
    err = err_ref[0:q, :]
    for p in range(pay_ref.shape[0]):
        pay_ref[p, 0:q, :] = err
        pay_ref[p, q : q + 1, :] = sums


def middle(err, got, chunk, items, peers):
    return pl.pallas_call(
        functools.partial(middle_kernel, chunk, items // 4),
        in_specs=whole(2),
        out_specs=whole(1)[0],
        out_shape=jax.ShapeDtypeStruct((peers, 8, LANES), F32),
        compiler_params=params(2),
        name="middle",
    )(err, got)


def final_kernel(horizon, item_count, store_count, base_ref, item_ref, one_ref, two_ref, out_ref, sgap_ref, igap_ref, err_ref):
    width, stores = base_ref.shape
    items = width // horizon
    peers = two_ref.shape[0]
    valid1 = lax.broadcasted_iota(jnp.int32, (1, LANES), 1) < horizon

    def group(x, k):
        if k:
            x = pltpu.roll(x, LANES - k * GROUP, axis=1)
        return jnp.where(valid1, x, 0.0)

    n = items // 4
    colp = one_ref[0, 0:n, :]
    for p in range(1, one_ref.shape[0]):
        colp = colp + one_ref[p, 0:n, :]
    col = jnp.concatenate([group(colp, k) for k in range(4)], axis=0)
    item_err = item_ref[...] - col

    q = stores // peers // 4
    sums = two_ref[0, q : q + 1, :]
    for p in range(1, peers):
        sums = sums + two_ref[p, q : q + 1, :]
    total = group(sums, 2)
    err_s = group(sums, 0) - total
    err_i = group(sums, 1) - total
    for p in range(peers):
        for k in range(4):
            r = (p * 4 + k) * q
            err_ref[r : r + q, :] = group(two_ref[p, 0:q, :], k)
    store_err = err_ref[...].T[:horizon]

    denominator = 1.0 + item_count + store_count
    shift_s = (err_s * (1.0 + store_count) - store_count * err_i) / denominator
    shift_i = ((1.0 + item_count) * err_i - item_count * err_s) / denominator
    item_shift = (item_err - shift_s) / (1.0 + store_count)
    columns = jnp.concatenate(
        [item_shift, shift_i, jnp.zeros((LANES - items - 1, LANES), F32)], axis=0
    ).T[:horizon]
    store_shift = (store_err - columns[:, items : items + 1]) / (1.0 + item_count)

    a = jnp.concatenate([store_shift, store_shift], axis=0)
    b = jnp.concatenate([columns, pltpu.roll(columns, LANES - 1, axis=1)], axis=0)
    for j in range(items // 2):
        rows = slice(2 * j * horizon, (2 * j + 2) * horizon)
        out_ref[rows, :] = base_ref[rows, :] + a + b[:, 2 * j : 2 * j + 1]
    sgap_ref[...] = store_err * (1.0 / math.sqrt(item_count))
    igap_ref[...] = item_err[:, :horizon] * (1.0 / math.sqrt(store_count))


def final(base, item_fc, one, two, horizon, item_count, store_count):
    width, stores = base.shape
    items = width // horizon
    return pl.pallas_call(
        functools.partial(final_kernel, horizon, item_count, store_count),
        in_specs=whole(4),
        out_specs=whole(3),
        out_shape=[
            jax.ShapeDtypeStruct((width, stores), F32),
            jax.ShapeDtypeStruct((horizon, stores), F32),
            jax.ShapeDtypeStruct((items, horizon), F32),
        ],
        scratch_shapes=[pltpu.VMEM((stores, LANES), F32)],
        compiler_params=params(6),
        name="final",
    )(base, item_fc, one, two)


def exchange(x, axis):
    return lax.all_to_all(x, axis, 0, 0, tiled=True)


def partner(x, axis, flip):
    return lax.ppermute(x, axis, [(i, i ^ flip) for i in range(lax.axis_size(axis))])


def add_over_x(x):
    x = x + partner(x, "store", 1)
    return x + partner(x, "store", 2)


def add_over_y(x):
    near, far, across = (partner(x, "store", flip) for flip in (4, 12, 8))
    return (x + across) + (near + far)


def body(history, w1, w2, final_layer_matrix):
    stores, items, _ = history.shape
    horizon = final_layer_matrix.shape[1]
    n_store, n_dept = lax.axis_size("store"), lax.axis_size("dept")
    chunk = stores // n_dept
    w3 = final_layer_matrix.T

    pay, item_part, col, y = bottom(history, w1, w2, w3, n_dept, stores // 4, stores // 8)
    store_parts = exchange(pay, "dept")
    item_hist = add_over_x(item_part)
    base = arrange(y, items, horizon)
    base, item_hist = lax.optimization_barrier((base, item_hist))
    item_hist = add_over_y(item_hist)
    err, item_fc, pay_one = totals(store_parts, item_hist, w1, w2, w3, col, chunk, n_store)
    one = exchange(pay_one, "store")
    pay_two = middle(err, one, chunk, items, n_dept)
    two = exchange(pay_two, "dept")
    out, store_gap, item_gap = final(
        base, item_fc, one, two, horizon, float(items * n_dept), float(stores * n_store)
    )
    return out.T, store_gap, item_gap.T


def solution(mesh):
    return jax.shard_map(
        body,
        mesh=mesh,
        in_specs=(P("store", "dept", None), P(), P(), P()),
        out_specs=(P("store", "dept"), P(None, "store"), P(None, "dept")),
        check_vma=False,
    )
```

```python
import functools
import math

import jax
import jax.numpy as jnp
from jax import lax
from jax.experimental import pallas as pl
from jax.experimental.pallas import tpu as pltpu
from jax.sharding import PartitionSpec as P

F32 = jnp.float32
BF16 = jnp.bfloat16
LANES = 128
GROUP = 32
MIB = 1024 * 1024


def whole(n):
    return [pl.BlockSpec(memory_space=pltpu.VMEM)] * n


def params(mib):
    return pltpu.CompilerParams(vmem_limit_bytes=mib * MIB)


def stay(x):
    return pltpu.with_memory_space_constraint(x, pltpu.HBM)


def relu(x):
    return jnp.maximum(x.astype(BF16), 0)


def forecaster(x, w1, w2, w3):
    var = jnp.sum(x * x, axis=-1, keepdims=True) * (1.0 / x.shape[-1]) + 1e-05
    inv = lax.rsqrt(var)
    z = (x * inv).astype(BF16)
    a = relu(jnp.dot(z, w1, preferred_element_type=F32))
    b = relu(jnp.dot(a, w2, preferred_element_type=F32))
    return jnp.dot(b, w3, preferred_element_type=F32) * (var * inv)


def sum_items(x):
    stores, items, width = x.shape
    x = x.reshape(stores, items // 8, 8, width)
    total = x[:, 0]
    for k in range(1, items // 8):
        total = total + x[:, k]
    v = total.reshape(stores // 8, 8, 8, width)
    row = lax.broadcasted_iota(jnp.int32, (1, 1, 8, width), 2)
    for bit in (4, 2, 1):
        low = lax.rem(lax.div(row, bit), 2) == 0
        a, b = v[:, :bit], v[:, bit:]
        there = jnp.where(low, b, a)
        up = pltpu.roll(there, bit, axis=2)
        if bit < 4:
            up = jnp.where(low, pltpu.roll(there, 8 - bit, axis=2), up)
        v = jnp.where(low, a, b) + up
    return v.reshape(stores, width)


def widen(w3_ref, w3_wide):
    horizon = w3_ref.shape[0]
    w3_wide[...] = jnp.zeros_like(w3_wide)
    w3_wide[:, :horizon] = w3_ref[...].astype(F32).T.astype(BF16)


def pack_rows(x):
    n = x.shape[0] // 4
    out = x[0:n]
    for k in range(1, 4):
        out = out + pltpu.roll(x[k * n : (k + 1) * n], k * GROUP, axis=1)
    return out


def bottom_kernel(chunk, part, h_ref, w1_ref, w2_ref, w3_ref, keep_ref, send_ref, item_ref, col_ref, y_ref, w3_wide):
    block, items, days = h_ref.shape
    even = lax.rem(lax.axis_index("dept"), 2) == 0
    step = pl.program_id(0)

    @pl.when(step == 0)
    def _():
        widen(w3_ref, w3_wide)
        item_ref[...] = jnp.zeros_like(item_ref)
        col_ref[...] = jnp.zeros_like(col_ref)
        y_ref[...] = jnp.zeros_like(y_ref)

    w1, w2, w3 = w1_ref[...], w2_ref[...], w3_wide[...]
    tiles = days // LANES
    for p in range(block // part):
        x = h_ref[p * part : (p + 1) * part].astype(F32)
        by_store = sum_items(x)
        item_ref[...] += jnp.sum(x, axis=0)
        y = forecaster(x.reshape(part * items, days), w1, w2, w3)
        y_ref[p * part * items : (p + 1) * part * items, :] += pltpu.roll(y, step * GROUP, axis=1)
        y = y.reshape(part, items, LANES)
        row = sum_items(y)
        col_ref[...] += jnp.sum(y, axis=0)
        for q in range(0, part // chunk, 2):
            pair = (p * (part // chunk) + q) // 2
            first, second = q * chunk, (q + 1) * chunk

            def put(where, a, b):
                keep_ref[pair, where, :] = jnp.where(even, a, b)
                send_ref[pair, where, :] = jnp.where(even, b, a)

            for t in range(tiles):
                day = slice(t * LANES, (t + 1) * LANES)
                put(
                    slice(t * chunk, (t + 1) * chunk),
                    by_store[first : first + chunk, day],
                    by_store[second : second + chunk, day],
                )
            put(
                slice(tiles * chunk, tiles * chunk + chunk // 4),
                pack_rows(row[first : first + chunk]),
                pack_rows(row[second : second + chunk]),
            )


def bottom(history, w1, w2, w3, peers, block, part):
    stores, items, days = history.shape
    hid = w1.shape[1]
    rows = stores * items
    chunk = stores // peers
    pay_rows = (days // LANES) * chunk + 8
    fixed = lambda shape: pl.BlockSpec(shape, lambda i: (0,) * len(shape))
    return pl.pallas_call(
        functools.partial(bottom_kernel, chunk, part),
        grid=(stores // block,),
        in_specs=[
            pl.BlockSpec((block, items, days), lambda i: (i, 0, 0)),
            fixed(w1.shape),
            fixed(w2.shape),
            fixed(w3.shape),
        ],
        out_specs=[
            pl.BlockSpec((block // chunk // 2, pay_rows, LANES), lambda i: (i, 0, 0)),
            pl.BlockSpec((block // chunk // 2, pay_rows, LANES), lambda i: (i, 0, 0)),
            fixed((items, days)),
            fixed((items, LANES)),
            fixed((block * items, LANES)),
        ],
        out_shape=[
            jax.ShapeDtypeStruct((peers // 2, pay_rows, LANES), F32),
            jax.ShapeDtypeStruct((peers // 2, pay_rows, LANES), F32),
            jax.ShapeDtypeStruct((items, days), F32),
            jax.ShapeDtypeStruct((items, LANES), F32),
            jax.ShapeDtypeStruct((block * items, LANES), F32),
        ],
        scratch_shapes=[pltpu.VMEM((hid, LANES), BF16)],
        compiler_params=params(24),
        cost_estimate=pl.CostEstimate(
            flops=2 * rows * (days * hid + hid * hid + hid * LANES),
            bytes_accessed=2 * history.size,
            transcendentals=0,
        ),
        name="bottom",
    )(stay(history), stay(w1), stay(w2), stay(w3))


def arrange_kernel(horizon, items, y_ref, out_ref):
    block = y_ref.shape[0] // items
    for i in range(items):
        v = y_ref[pl.ds(i, block, stride=items), :].T
        blocks = [v[k * GROUP : k * GROUP + horizon] for k in range(LANES // GROUP)]
        out_ref[i * horizon : (i + 1) * horizon, :] = jnp.concatenate(blocks, axis=1)


def arrange(y, items, horizon):
    rows = y.shape[0]
    stores = rows // items * (LANES // GROUP)
    return pl.pallas_call(
        functools.partial(arrange_kernel, horizon, items),
        in_specs=whole(1),
        out_specs=whole(1)[0],
        out_shape=jax.ShapeDtypeStruct((items * horizon, stores), F32),
        compiler_params=params(12),
        cost_estimate=pl.CostEstimate(
            flops=16 * rows * LANES, bytes_accessed=12 * rows * LANES, transcendentals=0
        ),
        name="arrange",
    )(y)


def totals_kernel(chunk, s_ref, i_ref, w1_ref, w2_ref, w3_ref, col_ref, err_ref, item_ref, pay_ref, w3_wide):
    days = w1_ref.shape[0]
    widen(w3_ref, w3_wide)
    got = s_ref[0]
    for p in range(1, s_ref.shape[0]):
        got = got + s_ref[p]
    tiles = days // LANES
    x = jnp.concatenate([got[t * chunk : (t + 1) * chunk] for t in range(tiles)], axis=1)
    x = jnp.concatenate([x, i_ref[...]], axis=0)
    y = forecaster(x, w1_ref[...], w2_ref[...], w3_wide[...])
    fc = y[:chunk]
    fi = y[chunk:]
    item_ref[...] = fi
    q = chunk // 4
    err_ref[0:q, :] = pack_rows(fc) - got[tiles * chunk : tiles * chunk + q]
    err_ref[q : q + 1, :] = pltpu.roll(jnp.sum(fi, axis=0, keepdims=True), GROUP, axis=1)
    col = col_ref[...]
    sums = jnp.sum(fc, axis=0, keepdims=True) + pltpu.roll(
        jnp.sum(col, axis=0, keepdims=True), 2 * GROUP, axis=1
    )
    packed = pack_rows(col)
    n = packed.shape[0]
    for p in range(pay_ref.shape[0]):
        pay_ref[p, 0:n, :] = packed
        pay_ref[p, n : n + 1, :] = sums


def totals(store_parts, item_hist, w1, w2, w3, col, chunk, item_peers):
    items = item_hist.shape[0]
    return pl.pallas_call(
        functools.partial(totals_kernel, chunk),
        in_specs=whole(6),
        out_specs=whole(3),
        out_shape=[
            jax.ShapeDtypeStruct((8, LANES), F32),
            jax.ShapeDtypeStruct((items, LANES), F32),
            jax.ShapeDtypeStruct((item_peers, 8, LANES), F32),
        ],
        scratch_shapes=[pltpu.VMEM((w1.shape[1], LANES), BF16)],
        compiler_params=params(8),
        name="totals",
    )(store_parts, item_hist, w1, w2, w3, col)


def middle_kernel(chunk, n, err_ref, got_ref, pay_ref):
    q = chunk // 4
    sums = err_ref[q : q + 1, :]
    for p in range(got_ref.shape[0]):
        sums = sums + got_ref[p, n : n + 1, :]
    err = err_ref[0:q, :]
    for p in range(pay_ref.shape[0]):
        pay_ref[p, 0:q, :] = err
        pay_ref[p, q : q + 1, :] = sums


def middle(err, got, chunk, items, peers):
    return pl.pallas_call(
        functools.partial(middle_kernel, chunk, items // 4),
        in_specs=whole(2),
        out_specs=whole(1)[0],
        out_shape=jax.ShapeDtypeStruct((peers, 8, LANES), F32),
        compiler_params=params(2),
        name="middle",
    )(err, got)


def final_kernel(horizon, item_count, store_count, base_ref, item_ref, one_ref, two_ref, out_ref, sgap_ref, igap_ref, err_ref):
    width, stores = base_ref.shape
    items = width // horizon
    peers = two_ref.shape[0]
    valid1 = lax.broadcasted_iota(jnp.int32, (1, LANES), 1) < horizon

    def group(x, k):
        if k:
            x = pltpu.roll(x, LANES - k * GROUP, axis=1)
        return jnp.where(valid1, x, 0.0)

    n = items // 4
    colp = one_ref[0, 0:n, :]
    for p in range(1, one_ref.shape[0]):
        colp = colp + one_ref[p, 0:n, :]
    col = jnp.concatenate([group(colp, k) for k in range(4)], axis=0)
    item_err = item_ref[...] - col

    q = stores // peers // 4
    sums = two_ref[0, q : q + 1, :]
    for p in range(1, peers):
        sums = sums + two_ref[p, q : q + 1, :]
    total = group(sums, 2)
    err_s = group(sums, 0) - total
    err_i = group(sums, 1) - total
    for p in range(peers):
        for k in range(4):
            r = (p * 4 + k) * q
            err_ref[r : r + q, :] = group(two_ref[p, 0:q, :], k)
    store_err = err_ref[...].T[:horizon]

    denominator = 1.0 + item_count + store_count
    shift_s = (err_s * (1.0 + store_count) - store_count * err_i) / denominator
    shift_i = ((1.0 + item_count) * err_i - item_count * err_s) / denominator
    item_shift = (item_err - shift_s) / (1.0 + store_count)
    columns = jnp.concatenate(
        [item_shift, shift_i, jnp.zeros((LANES - items - 1, LANES), F32)], axis=0
    ).T[:horizon]
    store_shift = (store_err - columns[:, items : items + 1]) / (1.0 + item_count)

    a = jnp.concatenate([store_shift, store_shift], axis=0)
    b = jnp.concatenate([columns, pltpu.roll(columns, LANES - 1, axis=1)], axis=0)
    for j in range(items // 2):
        rows = slice(2 * j * horizon, (2 * j + 2) * horizon)
        out_ref[rows, :] = base_ref[rows, :] + a + b[:, 2 * j : 2 * j + 1]
    sgap_ref[...] = store_err * (1.0 / math.sqrt(item_count))
    igap_ref[...] = item_err[:, :horizon] * (1.0 / math.sqrt(store_count))


def final(base, item_fc, one, two, horizon, item_count, store_count):
    width, stores = base.shape
    items = width // horizon
    return pl.pallas_call(
        functools.partial(final_kernel, horizon, item_count, store_count),
        in_specs=whole(4),
        out_specs=whole(3),
        out_shape=[
            jax.ShapeDtypeStruct((width, stores), F32),
            jax.ShapeDtypeStruct((horizon, stores), F32),
            jax.ShapeDtypeStruct((items, horizon), F32),
        ],
        scratch_shapes=[pltpu.VMEM((stores, LANES), F32)],
        compiler_params=params(6),
        name="final",
    )(base, item_fc, one, two)


def exchange(x, axis, groups=None):
    return lax.all_to_all(x, axis, 0, 0, axis_index_groups=groups, tiled=True)


def partner(x, axis, flip):
    return lax.ppermute(x, axis, [(i, i ^ flip) for i in range(lax.axis_size(axis))])


def add_over_x(x):
    x = x + partner(x, "store", 1)
    return x + partner(x, "store", 2)


def add_over_y(x):
    near, far, across = (partner(x, "store", flip) for flip in (4, 12, 8))
    return (x + across) + (near + far)


def body(history, w1, w2, final_layer_matrix):
    stores, items, _ = history.shape
    horizon = final_layer_matrix.shape[1]
    n_store, n_dept = lax.axis_size("store"), lax.axis_size("dept")
    chunk = stores // n_dept
    w3 = final_layer_matrix.T

    keep, send, item_part, col, y = bottom(history, w1, w2, w3, n_dept, stores // 4, stores // 8)
    came = partner(send, "dept", 1)
    item_hist = add_over_x(item_part)
    base = arrange(y, items, horizon)
    came, item_hist, base = lax.optimization_barrier((came, item_hist, base))
    along_z = [list(range(k, n_dept, 2)) for k in range(2)]
    store_parts = exchange(keep + came, "dept", along_z)
    item_hist = add_over_y(item_hist)
    err, item_fc, pay_one = totals(store_parts, item_hist, w1, w2, w3, col, chunk, n_store)
    one = exchange(pay_one, "store")
    pay_two = middle(err, one, chunk, items, n_dept)
    two = exchange(pay_two, "dept")
    out, store_gap, item_gap = final(
        base, item_fc, one, two, horizon, float(items * n_dept), float(stores * n_store)
    )
    return out.T, store_gap, item_gap.T


def solution(mesh):
    return jax.shard_map(
        body,
        mesh=mesh,
        in_specs=(P("store", "dept", None), P(), P(), P()),
        out_specs=(P("store", "dept"), P(None, "store"), P(None, "dept")),
        check_vma=False,
    )
```

```python
import functools
import math

import jax
import jax.numpy as jnp
from jax import lax
from jax.experimental import pallas as pl
from jax.experimental.pallas import tpu as pltpu
from jax.sharding import PartitionSpec as P

F32 = jnp.float32
BF16 = jnp.bfloat16
LANES = 128
GROUP = 32
MIB = 1024 * 1024


def whole(n):
    return [pl.BlockSpec(memory_space=pltpu.VMEM)] * n


def params(mib):
    return pltpu.CompilerParams(vmem_limit_bytes=mib * MIB)


def stay(x):
    return pltpu.with_memory_space_constraint(x, pltpu.HBM)


def relu(x):
    return jnp.maximum(x.astype(BF16), 0)


def forecaster(x, w1, w2, w3):
    var = jnp.sum(x * x, axis=-1, keepdims=True) * (1.0 / x.shape[-1]) + 1e-05
    inv = lax.rsqrt(var)
    z = (x * inv).astype(BF16)
    a = relu(jnp.dot(z, w1, preferred_element_type=F32))
    b = relu(jnp.dot(a, w2, preferred_element_type=F32))
    return jnp.dot(b, w3, preferred_element_type=F32) * (var * inv)


def sum_items(x):
    stores, items, width = x.shape
    x = x.reshape(stores, items // 8, 8, width)
    total = x[:, 0]
    for k in range(1, items // 8):
        total = total + x[:, k]
    v = total.reshape(stores // 8, 8, 8, width)
    row = lax.broadcasted_iota(jnp.int32, (1, 1, 8, width), 2)
    for bit in (4, 2, 1):
        low = lax.rem(lax.div(row, bit), 2) == 0
        a, b = v[:, :bit], v[:, bit:]
        there = jnp.where(low, b, a)
        up = pltpu.roll(there, bit, axis=2)
        if bit < 4:
            up = jnp.where(low, pltpu.roll(there, 8 - bit, axis=2), up)
        v = jnp.where(low, a, b) + up
    return v.reshape(stores, width)


def widen(w3_ref, w3_wide):
    horizon = w3_ref.shape[0]
    w3_wide[...] = jnp.zeros_like(w3_wide)
    w3_wide[:, :horizon] = w3_ref[...].astype(F32).T.astype(BF16)


def pack_rows(x):
    n = x.shape[0] // 4
    out = x[0:n]
    for k in range(1, 4):
        out = out + pltpu.roll(x[k * n : (k + 1) * n], k * GROUP, axis=1)
    return out


def bottom_kernel(chunk, part, h_ref, w1_ref, w2_ref, w3_ref, keep_ref, send_ref, item_ref, col_ref, y_ref, w3_wide):
    block, items, days = h_ref.shape
    even = lax.rem(lax.axis_index("dept"), 2) == 0
    step = pl.program_id(0)

    @pl.when(step == 0)
    def _():
        widen(w3_ref, w3_wide)
        item_ref[...] = jnp.zeros_like(item_ref)
        col_ref[...] = jnp.zeros_like(col_ref)
        y_ref[...] = jnp.zeros_like(y_ref)

    w1, w2, w3 = w1_ref[...], w2_ref[...], w3_wide[...]
    tiles = days // LANES
    for p in range(block // part):
        x = h_ref[p * part : (p + 1) * part].astype(F32)
        by_store = sum_items(x)
        item_ref[...] += jnp.sum(x, axis=0)
        y = forecaster(x.reshape(part * items, days), w1, w2, w3)
        y_ref[p * part * items : (p + 1) * part * items, :] += pltpu.roll(y, step * GROUP, axis=1)
        y = y.reshape(part, items, LANES)
        row = sum_items(y)
        col_ref[...] += jnp.sum(y, axis=0)
        for q in range(0, part // chunk, 2):
            pair = (p * (part // chunk) + q) // 2
            first, second = q * chunk, (q + 1) * chunk

            def put(where, a, b):
                keep_ref[pair, where, :] = jnp.where(even, a, b)
                send_ref[pair, where, :] = jnp.where(even, b, a)

            for t in range(tiles):
                day = slice(t * LANES, (t + 1) * LANES)
                put(
                    slice(t * chunk, (t + 1) * chunk),
                    by_store[first : first + chunk, day],
                    by_store[second : second + chunk, day],
                )
            put(
                slice(tiles * chunk, tiles * chunk + chunk // 4),
                pack_rows(row[first : first + chunk]),
                pack_rows(row[second : second + chunk]),
            )


def bottom(history, w1, w2, w3, peers, block, part):
    stores, items, days = history.shape
    hid = w1.shape[1]
    rows = stores * items
    chunk = stores // peers
    pay_rows = (days // LANES) * chunk + 8
    fixed = lambda shape: pl.BlockSpec(shape, lambda i: (0,) * len(shape))
    return pl.pallas_call(
        functools.partial(bottom_kernel, chunk, part),
        grid=(stores // block,),
        in_specs=[
            pl.BlockSpec((block, items, days), lambda i: (i, 0, 0)),
            fixed(w1.shape),
            fixed(w2.shape),
            fixed(w3.shape),
        ],
        out_specs=[
            pl.BlockSpec((block // chunk // 2, pay_rows, LANES), lambda i: (i, 0, 0)),
            pl.BlockSpec((block // chunk // 2, pay_rows, LANES), lambda i: (i, 0, 0)),
            fixed((items, days)),
            fixed((items, LANES)),
            fixed((block * items, LANES)),
        ],
        out_shape=[
            jax.ShapeDtypeStruct((peers // 2, pay_rows, LANES), F32),
            jax.ShapeDtypeStruct((peers // 2, pay_rows, LANES), F32),
            jax.ShapeDtypeStruct((items, days), F32),
            jax.ShapeDtypeStruct((items, LANES), F32),
            jax.ShapeDtypeStruct((block * items, LANES), F32),
        ],
        scratch_shapes=[pltpu.VMEM((hid, LANES), BF16)],
        compiler_params=params(24),
        cost_estimate=pl.CostEstimate(
            flops=2 * rows * (days * hid + hid * hid + hid * LANES),
            bytes_accessed=2 * history.size,
            transcendentals=0,
        ),
        name="bottom",
    )(stay(history), stay(w1), stay(w2), stay(w3))


def arrange_kernel(horizon, items, y_ref, out_ref):
    block = y_ref.shape[0] // items
    for i in range(items):
        v = y_ref[pl.ds(i, block, stride=items), :].T
        blocks = [v[k * GROUP : k * GROUP + horizon] for k in range(LANES // GROUP)]
        out_ref[i * horizon : (i + 1) * horizon, :] = jnp.concatenate(blocks, axis=1)


def arrange(y, items, horizon):
    rows = y.shape[0]
    stores = rows // items * (LANES // GROUP)
    return pl.pallas_call(
        functools.partial(arrange_kernel, horizon, items),
        in_specs=whole(1),
        out_specs=whole(1)[0],
        out_shape=jax.ShapeDtypeStruct((items * horizon, stores), F32),
        compiler_params=params(12),
        cost_estimate=pl.CostEstimate(
            flops=16 * rows * LANES, bytes_accessed=12 * rows * LANES, transcendentals=0
        ),
        name="arrange",
    )(y)


def totals_kernel(chunk, s_ref, i_ref, w1_ref, w2_ref, w3_ref, col_ref, err_ref, item_ref, pay_ref, w3_wide):
    days = w1_ref.shape[0]
    widen(w3_ref, w3_wide)
    got = s_ref[0]
    for p in range(1, s_ref.shape[0]):
        got = got + s_ref[p]
    tiles = days // LANES
    x = jnp.concatenate([got[t * chunk : (t + 1) * chunk] for t in range(tiles)], axis=1)
    x = jnp.concatenate([x, i_ref[...]], axis=0)
    y = forecaster(x, w1_ref[...], w2_ref[...], w3_wide[...])
    fc = y[:chunk]
    fi = y[chunk:]
    item_ref[...] = fi
    q = chunk // 4
    err_ref[0:q, :] = pack_rows(fc) - got[tiles * chunk : tiles * chunk + q]
    err_ref[q : q + 1, :] = pltpu.roll(jnp.sum(fi, axis=0, keepdims=True), GROUP, axis=1)
    col = col_ref[...]
    sums = jnp.sum(fc, axis=0, keepdims=True) + pltpu.roll(
        jnp.sum(col, axis=0, keepdims=True), 2 * GROUP, axis=1
    )
    packed = pack_rows(col)
    n = packed.shape[0]
    for p in range(pay_ref.shape[0]):
        pay_ref[p, 0:n, :] = packed
        pay_ref[p, n : n + 1, :] = sums


def totals(store_parts, item_hist, w1, w2, w3, col, chunk, item_peers):
    items = item_hist.shape[0]
    return pl.pallas_call(
        functools.partial(totals_kernel, chunk),
        in_specs=whole(6),
        out_specs=whole(3),
        out_shape=[
            jax.ShapeDtypeStruct((8, LANES), F32),
            jax.ShapeDtypeStruct((items, LANES), F32),
            jax.ShapeDtypeStruct((item_peers, 8, LANES), F32),
        ],
        scratch_shapes=[pltpu.VMEM((w1.shape[1], LANES), BF16)],
        compiler_params=params(8),
        name="totals",
    )(store_parts, item_hist, w1, w2, w3, col)


def middle_kernel(chunk, n, err_ref, got_ref, pay_ref):
    q = chunk // 4
    sums = err_ref[q : q + 1, :]
    for p in range(got_ref.shape[0]):
        sums = sums + got_ref[p, n : n + 1, :]
    err = err_ref[0:q, :]
    for p in range(pay_ref.shape[0]):
        pay_ref[p, 0:q, :] = err
        pay_ref[p, q : q + 1, :] = sums


def middle(err, got, chunk, items, peers):
    return pl.pallas_call(
        functools.partial(middle_kernel, chunk, items // 4),
        in_specs=whole(2),
        out_specs=whole(1)[0],
        out_shape=jax.ShapeDtypeStruct((peers, 8, LANES), F32),
        compiler_params=params(2),
        name="middle",
    )(err, got)


def final_kernel(horizon, item_count, store_count, base_ref, item_ref, one_ref, two_ref, out_ref, sgap_ref, igap_ref, err_ref):
    width, stores = base_ref.shape
    items = width // horizon
    peers = two_ref.shape[0]
    valid1 = lax.broadcasted_iota(jnp.int32, (1, LANES), 1) < horizon

    def group(x, k):
        if k:
            x = pltpu.roll(x, LANES - k * GROUP, axis=1)
        return jnp.where(valid1, x, 0.0)

    n = items // 4
    colp = one_ref[0, 0:n, :]
    for p in range(1, one_ref.shape[0]):
        colp = colp + one_ref[p, 0:n, :]
    col = jnp.concatenate([group(colp, k) for k in range(4)], axis=0)
    item_err = item_ref[...] - col

    q = stores // peers // 4
    sums = two_ref[0, q : q + 1, :]
    for p in range(1, peers):
        sums = sums + two_ref[p, q : q + 1, :]
    total = group(sums, 2)
    err_s = group(sums, 0) - total
    err_i = group(sums, 1) - total
    for p in range(peers):
        for k in range(4):
            r = (p * 4 + k) * q
            err_ref[r : r + q, :] = group(two_ref[p, 0:q, :], k)
    store_err = err_ref[...].T[:horizon]

    denominator = 1.0 + item_count + store_count
    shift_s = (err_s * (1.0 + store_count) - store_count * err_i) / denominator
    shift_i = ((1.0 + item_count) * err_i - item_count * err_s) / denominator
    item_shift = (item_err - shift_s) / (1.0 + store_count)
    columns = jnp.concatenate(
        [item_shift, shift_i, jnp.zeros((LANES - items - 1, LANES), F32)], axis=0
    ).T[:horizon]
    store_shift = (store_err - columns[:, items : items + 1]) / (1.0 + item_count)

    a = jnp.concatenate([store_shift, store_shift], axis=0)
    b = jnp.concatenate([columns, pltpu.roll(columns, LANES - 1, axis=1)], axis=0)
    for j in range(items // 2):
        rows = slice(2 * j * horizon, (2 * j + 2) * horizon)
        out_ref[rows, :] = base_ref[rows, :] + a + b[:, 2 * j : 2 * j + 1]
    sgap_ref[...] = store_err * (1.0 / math.sqrt(item_count))
    igap_ref[...] = item_err[:, :horizon] * (1.0 / math.sqrt(store_count))


def final(base, item_fc, one, two, horizon, item_count, store_count):
    width, stores = base.shape
    items = width // horizon
    return pl.pallas_call(
        functools.partial(final_kernel, horizon, item_count, store_count),
        in_specs=whole(4),
        out_specs=whole(3),
        out_shape=[
            jax.ShapeDtypeStruct((width, stores), F32),
            jax.ShapeDtypeStruct((horizon, stores), F32),
            jax.ShapeDtypeStruct((items, horizon), F32),
        ],
        scratch_shapes=[pltpu.VMEM((stores, LANES), F32)],
        compiler_params=params(6),
        name="final",
    )(base, item_fc, one, two)


def exchange(x, axis, groups=None):
    return lax.all_to_all(x, axis, 0, 0, axis_index_groups=groups, tiled=True)


def partner(x, axis, flip):
    return lax.ppermute(x, axis, [(i, i ^ flip) for i in range(lax.axis_size(axis))])


def add_over_y(x):
    near, far, across = (partner(x, "store", flip) for flip in (4, 12, 8))
    return (x + across) + (near + far)


def body(history, w1, w2, final_layer_matrix):
    stores, items, _ = history.shape
    horizon = final_layer_matrix.shape[1]
    n_store, n_dept = lax.axis_size("store"), lax.axis_size("dept")
    chunk = stores // n_dept
    w3 = final_layer_matrix.T

    keep, send, item_part, col, y = bottom(history, w1, w2, w3, n_dept, stores // 4, stores // 8)
    came = partner(send, "dept", 1)
    item_hist = add_over_y(item_part + partner(item_part, "store", 1))
    base = arrange(y, items, horizon)
    came, item_hist, base = lax.optimization_barrier((came, item_hist, base))
    along_z = [list(range(k, n_dept, 2)) for k in range(2)]
    store_parts = exchange(keep + came, "dept", along_z)
    item_hist = item_hist + partner(item_hist, "store", 2)
    err, item_fc, pay_one = totals(store_parts, item_hist, w1, w2, w3, col, chunk, n_store)
    one = exchange(pay_one, "store")
    pay_two = middle(err, one, chunk, items, n_dept)
    two = exchange(pay_two, "dept")
    out, store_gap, item_gap = final(
        base, item_fc, one, two, horizon, float(items * n_dept), float(stores * n_store)
    )
    return out.T, store_gap, item_gap.T


def solution(mesh):
    return jax.shard_map(
        body,
        mesh=mesh,
        in_specs=(P("store", "dept", None), P(), P(), P()),
        out_specs=(P("store", "dept"), P(None, "store"), P(None, "dept")),
        check_vma=False,
    )
```

```python
import functools
import math

import jax
import jax.numpy as jnp
from jax import lax
from jax.experimental import pallas as pl
from jax.experimental.pallas import tpu as pltpu
from jax.sharding import PartitionSpec as P

F32 = jnp.float32
BF16 = jnp.bfloat16
LANES = 128
GROUP = 32
MIB = 1024 * 1024
PIECES = 3


def whole(n):
    return [pl.BlockSpec(memory_space=pltpu.VMEM)] * n


def params(mib):
    return pltpu.CompilerParams(vmem_limit_bytes=mib * MIB)


def stay(x):
    return pltpu.with_memory_space_constraint(x, pltpu.HBM)


def relu(x):
    return jnp.maximum(x.astype(BF16), 0)


def forecaster(x, w1, w2, w3):
    var = jnp.sum(x * x, axis=-1, keepdims=True) * (1.0 / x.shape[-1]) + 1e-05
    inv = lax.rsqrt(var)
    z = (x * inv).astype(BF16)
    a = relu(jnp.dot(z, w1, preferred_element_type=F32))
    b = relu(jnp.dot(a, w2, preferred_element_type=F32))
    return jnp.dot(b, w3, preferred_element_type=F32) * (var * inv)


def sum_items(x):
    stores, items, width = x.shape
    x = x.reshape(stores, items // 8, 8, width)
    total = x[:, 0]
    for k in range(1, items // 8):
        total = total + x[:, k]
    v = total.reshape(stores // 8, 8, 8, width)
    row = lax.broadcasted_iota(jnp.int32, (1, 1, 8, width), 2)
    for bit in (4, 2, 1):
        low = lax.rem(lax.div(row, bit), 2) == 0
        a, b = v[:, :bit], v[:, bit:]
        there = jnp.where(low, b, a)
        up = pltpu.roll(there, bit, axis=2)
        if bit < 4:
            up = jnp.where(low, pltpu.roll(there, 8 - bit, axis=2), up)
        v = jnp.where(low, a, b) + up
    return v.reshape(stores, width)


def widen(w3_ref, w3_wide):
    horizon = w3_ref.shape[0]
    w3_wide[...] = jnp.zeros_like(w3_wide)
    w3_wide[:, :horizon] = w3_ref[...].astype(F32).T.astype(BF16)


def pack_rows(x):
    n = x.shape[0] // 4
    out = x[0:n]
    for k in range(1, 4):
        out = out + pltpu.roll(x[k * n : (k + 1) * n], k * GROUP, axis=1)
    return out


def bottom_kernel(chunk, part, h_ref, w1_ref, w2_ref, w3_ref, pay_ref, item_ref, col_ref, y_ref, w1_out, w2_out, w3_wide):
    block, items, days = h_ref.shape
    step = pl.program_id(0)

    @pl.when(step == 0)
    def _():
        widen(w3_ref, w3_wide)
        item_ref[...] = jnp.zeros_like(item_ref)
        col_ref[...] = jnp.zeros_like(col_ref)
        y_ref[...] = jnp.zeros_like(y_ref)
        w1_out[...] = w1_ref[...]
        w2_out[...] = w2_ref[...]

    w1, w2, w3 = w1_ref[...], w2_ref[...], w3_wide[...]
    tiles = days // LANES
    for p in range(block // part):
        x = h_ref[p * part : (p + 1) * part].astype(F32)
        by_store = sum_items(x)
        item_ref[...] += jnp.sum(x, axis=0)
        y = forecaster(x.reshape(part * items, days), w1, w2, w3)
        y_ref[p * part * items : (p + 1) * part * items, :] += pltpu.roll(y, step * GROUP, axis=1)
        y = y.reshape(part, items, LANES)
        row = sum_items(y)
        col_ref[...] += jnp.sum(y, axis=0)
        for q in range(part // chunk):
            peer = p * (part // chunk) + q
            for t in range(tiles):
                pay_ref[peer, t * chunk : (t + 1) * chunk, :] = by_store[
                    q * chunk : (q + 1) * chunk, t * LANES : (t + 1) * LANES
                ]
            pay_ref[peer, tiles * chunk : tiles * chunk + chunk // 4, :] = pack_rows(
                row[q * chunk : (q + 1) * chunk]
            )


def bottom(history, w1, w2, w3, peers, block, part):
    stores, items, days = history.shape
    hid = w1.shape[1]
    rows = stores * items
    chunk = stores // peers
    pay_rows = (days // LANES) * chunk + 8
    fixed = lambda shape: pl.BlockSpec(shape, lambda i: (0,) * len(shape))
    return pl.pallas_call(
        functools.partial(bottom_kernel, chunk, part),
        grid=(stores // block,),
        in_specs=[
            pl.BlockSpec((block, items, days), lambda i: (i, 0, 0)),
            fixed(w1.shape),
            fixed(w2.shape),
            fixed(w3.shape),
        ],
        out_specs=[
            pl.BlockSpec((block // chunk, pay_rows, LANES), lambda i: (i, 0, 0)),
            fixed((items, days)),
            fixed((items, LANES)),
            fixed((block * items, LANES)),
            fixed(w1.shape),
            fixed(w2.shape),
        ],
        out_shape=[
            jax.ShapeDtypeStruct((peers, pay_rows, LANES), F32),
            jax.ShapeDtypeStruct((items, days), F32),
            jax.ShapeDtypeStruct((items, LANES), F32),
            jax.ShapeDtypeStruct((block * items, LANES), F32),
            jax.ShapeDtypeStruct(w1.shape, BF16),
            jax.ShapeDtypeStruct(w2.shape, BF16),
        ],
        scratch_shapes=[pltpu.VMEM((hid, LANES), BF16)],
        compiler_params=params(24),
        cost_estimate=pl.CostEstimate(
            flops=2 * rows * (days * hid + hid * hid + hid * LANES),
            bytes_accessed=2 * history.size,
            transcendentals=0,
        ),
        name="bottom",
    )(stay(history), stay(w1), stay(w2), stay(w3))


def arrange_kernel(horizon, items, y_ref, out_ref):
    block = y_ref.shape[0] // items
    for i in range(items):
        v = y_ref[pl.ds(i, block, stride=items), :].T
        blocks = [v[k * GROUP : k * GROUP + horizon] for k in range(LANES // GROUP)]
        out_ref[i * horizon : (i + 1) * horizon, :] = jnp.concatenate(blocks, axis=1)


def arrange(y, items, horizon):
    rows = y.shape[0]
    stores = rows // items * (LANES // GROUP)
    return pl.pallas_call(
        functools.partial(arrange_kernel, horizon, items),
        in_specs=whole(1),
        out_specs=whole(1)[0],
        out_shape=jax.ShapeDtypeStruct((items * horizon, stores), F32),
        compiler_params=params(12),
        cost_estimate=pl.CostEstimate(
            flops=16 * rows * LANES, bytes_accessed=12 * rows * LANES, transcendentals=0
        ),
        name="arrange",
    )(y)


def totals_kernel(chunk, s_ref, i_ref, w1_ref, w2_ref, w3_ref, col_ref, err_ref, item_ref, pay_ref, w3_wide):
    days = w1_ref.shape[0]
    widen(w3_ref, w3_wide)
    got = s_ref[0]
    for p in range(1, s_ref.shape[0]):
        got = got + s_ref[p]
    tiles = days // LANES
    x = jnp.concatenate([got[t * chunk : (t + 1) * chunk] for t in range(tiles)], axis=1)
    x = jnp.concatenate([x, i_ref[...]], axis=0)
    y = forecaster(x, w1_ref[...], w2_ref[...], w3_wide[...])
    fc = y[:chunk]
    fi = y[chunk:]
    item_ref[...] = fi
    q = chunk // 4
    err_ref[0:q, :] = pack_rows(fc) - got[tiles * chunk : tiles * chunk + q]
    err_ref[q : q + 1, :] = pltpu.roll(jnp.sum(fi, axis=0, keepdims=True), GROUP, axis=1)
    col = col_ref[...]
    sums = jnp.sum(fc, axis=0, keepdims=True) + pltpu.roll(
        jnp.sum(col, axis=0, keepdims=True), 2 * GROUP, axis=1
    )
    packed = pack_rows(col)
    n = packed.shape[0]
    for p in range(pay_ref.shape[0]):
        pay_ref[p, 0:n, :] = packed
        pay_ref[p, n : n + 1, :] = sums


def totals(store_parts, item_hist, w1, w2, w3, col, chunk, item_peers):
    items = item_hist.shape[0]
    return pl.pallas_call(
        functools.partial(totals_kernel, chunk),
        in_specs=whole(6),
        out_specs=whole(3),
        out_shape=[
            jax.ShapeDtypeStruct((8, LANES), F32),
            jax.ShapeDtypeStruct((items, LANES), F32),
            jax.ShapeDtypeStruct((item_peers, 8, LANES), F32),
        ],
        scratch_shapes=[pltpu.VMEM((w1.shape[1], LANES), BF16)],
        compiler_params=params(8),
        name="totals",
    )(store_parts, item_hist, w1, w2, w3, col)


def middle_kernel(chunk, n, err_ref, got_ref, pay_ref):
    q = chunk // 4
    sums = err_ref[q : q + 1, :]
    for p in range(got_ref.shape[0]):
        sums = sums + got_ref[p, n : n + 1, :]
    err = err_ref[0:q, :]
    for p in range(pay_ref.shape[0]):
        pay_ref[p, 0:q, :] = err
        pay_ref[p, q : q + 1, :] = sums


def middle(err, got, chunk, items, peers):
    return pl.pallas_call(
        functools.partial(middle_kernel, chunk, items // 4),
        in_specs=whole(2),
        out_specs=whole(1)[0],
        out_shape=jax.ShapeDtypeStruct((peers, 8, LANES), F32),
        compiler_params=params(2),
        name="middle",
    )(err, got)


def final_kernel(horizon, item_count, store_count, base_ref, item_ref, one_ref, two_ref, out_hbm, sgap_ref, igap_ref, err_ref, out_ref, sem):
    width, stores = base_ref.shape
    items = width // horizon
    peers = two_ref.shape[0]
    valid1 = lax.broadcasted_iota(jnp.int32, (1, LANES), 1) < horizon

    def group(x, k):
        if k:
            x = pltpu.roll(x, LANES - k * GROUP, axis=1)
        return jnp.where(valid1, x, 0.0)

    n = items // 4
    colp = one_ref[0, 0:n, :]
    for p in range(1, one_ref.shape[0]):
        colp = colp + one_ref[p, 0:n, :]
    col = jnp.concatenate([group(colp, k) for k in range(4)], axis=0)
    item_err = item_ref[...] - col

    q = stores // peers // 4
    sums = two_ref[0, q : q + 1, :]
    for p in range(1, peers):
        sums = sums + two_ref[p, q : q + 1, :]
    total = group(sums, 2)
    err_s = group(sums, 0) - total
    err_i = group(sums, 1) - total
    for p in range(peers):
        for k in range(4):
            r = (p * 4 + k) * q
            err_ref[r : r + q, :] = group(two_ref[p, 0:q, :], k)
    store_err = err_ref[...].T[:horizon]

    denominator = 1.0 + item_count + store_count
    shift_s = (err_s * (1.0 + store_count) - store_count * err_i) / denominator
    shift_i = ((1.0 + item_count) * err_i - item_count * err_s) / denominator
    item_shift = (item_err - shift_s) / (1.0 + store_count)
    columns = jnp.concatenate(
        [item_shift, shift_i, jnp.zeros((LANES - items - 1, LANES), F32)], axis=0
    ).T[:horizon]
    store_shift = (store_err - columns[:, items : items + 1]) / (1.0 + item_count)

    a = jnp.concatenate([store_shift, store_shift], axis=0)
    b = jnp.concatenate([columns, pltpu.roll(columns, LANES - 1, axis=1)], axis=0)
    each = items // 2 // PIECES
    copies = []
    for j in range(items // 2):
        rows = slice(2 * j * horizon, (2 * j + 2) * horizon)
        out_ref[rows, :] = base_ref[rows, :] + a + b[:, 2 * j : 2 * j + 1]
        if (j + 1) % each == 0:
            piece = pl.ds((j + 1 - each) * 2 * horizon, each * 2 * horizon)
            copy = pltpu.make_async_copy(out_ref.at[piece], out_hbm.at[piece], sem.at[j // each])
            copy.start()
            copies.append(copy)
    sgap_ref[...] = store_err * (1.0 / math.sqrt(item_count))
    igap_ref[...] = item_err[:, :horizon] * (1.0 / math.sqrt(store_count))
    for copy in copies:
        copy.wait()


def final(base, item_fc, one, two, horizon, item_count, store_count):
    width, stores = base.shape
    items = width // horizon
    return pl.pallas_call(
        functools.partial(final_kernel, horizon, item_count, store_count),
        in_specs=whole(4),
        out_specs=[pl.BlockSpec(memory_space=pltpu.HBM)] + whole(2),
        out_shape=[
            pltpu.HBM((width, stores), F32),
            jax.ShapeDtypeStruct((horizon, stores), F32),
            jax.ShapeDtypeStruct((items, horizon), F32),
        ],
        scratch_shapes=[
            pltpu.VMEM((stores, LANES), F32),
            pltpu.VMEM((width, stores), F32),
            pltpu.SemaphoreType.DMA((PIECES,)),
        ],
        compiler_params=params(6),
        name="final",
    )(base, item_fc, one, two)


def exchange(x, axis):
    return lax.all_to_all(x, axis, 0, 0, tiled=True)


def partner(x, axis, flip):
    return lax.ppermute(x, axis, [(i, i ^ flip) for i in range(lax.axis_size(axis))])


def add_over_x(x):
    x = x + partner(x, "store", 1)
    return x + partner(x, "store", 2)


def add_over_y(x):
    near, far, across = (partner(x, "store", flip) for flip in (4, 12, 8))
    return (x + across) + (near + far)


def body(history, w1, w2, final_layer_matrix):
    stores, items, _ = history.shape
    horizon = final_layer_matrix.shape[1]
    n_store, n_dept = lax.axis_size("store"), lax.axis_size("dept")
    chunk = stores // n_dept
    w3 = final_layer_matrix.T

    pay, item_part, col, y, w1_near, w2_near = bottom(history, w1, w2, w3, n_dept, stores // 4, stores // 8)
    store_parts = exchange(pay, "dept")
    item_hist = add_over_x(item_part)
    base = arrange(y, items, horizon)
    base, item_hist = lax.optimization_barrier((base, item_hist))
    item_hist = add_over_y(item_hist)
    err, item_fc, pay_one = totals(store_parts, item_hist, w1_near, w2_near, w3, col, chunk, n_store)
    one = exchange(pay_one, "store")
    pay_two = middle(err, one, chunk, items, n_dept)
    two = exchange(pay_two, "dept")
    out, store_gap, item_gap = final(
        base, item_fc, one, two, horizon, float(items * n_dept), float(stores * n_store)
    )
    return out.T, store_gap, item_gap.T


def solution(mesh):
    return jax.shard_map(
        body,
        mesh=mesh,
        in_specs=(P("store", "dept", None), P(), P(), P()),
        out_specs=(P("store", "dept"), P(None, "store"), P(None, "dept")),
        check_vma=False,
    )
```

```python
import functools
import math

import jax
import jax.numpy as jnp
from jax import lax
from jax.experimental import pallas as pl
from jax.experimental.pallas import tpu as pltpu
from jax.sharding import PartitionSpec as P

F32 = jnp.float32
BF16 = jnp.bfloat16
LANES = 128
GROUP = 32
MIB = 1024 * 1024


def whole(n):
    return [pl.BlockSpec(memory_space=pltpu.VMEM)] * n


def params(mib):
    return pltpu.CompilerParams(vmem_limit_bytes=mib * MIB)


def stay(x):
    return pltpu.with_memory_space_constraint(x, pltpu.HBM)


def relu(x):
    return jnp.maximum(x.astype(BF16), 0)


def forecaster(x, w1, w2, w3):
    var = jnp.sum(x * x, axis=-1, keepdims=True) * (1.0 / x.shape[-1]) + 1e-05
    inv = lax.rsqrt(var)
    z = (x * inv).astype(BF16)
    a = relu(jnp.dot(z, w1, preferred_element_type=F32))
    b = relu(jnp.dot(a, w2, preferred_element_type=F32))
    return jnp.dot(b, w3, preferred_element_type=F32) * (var * inv)


def sum_items(x):
    stores, items, width = x.shape
    x = x.reshape(stores, items // 8, 8, width)
    total = x[:, 0]
    for k in range(1, items // 8):
        total = total + x[:, k]
    v = total.reshape(stores // 8, 8, 8, width)
    row = lax.broadcasted_iota(jnp.int32, (1, 1, 8, width), 2)
    for bit in (4, 2, 1):
        low = lax.rem(lax.div(row, bit), 2) == 0
        a, b = v[:, :bit], v[:, bit:]
        there = jnp.where(low, b, a)
        up = pltpu.roll(there, bit, axis=2)
        if bit < 4:
            up = jnp.where(low, pltpu.roll(there, 8 - bit, axis=2), up)
        v = jnp.where(low, a, b) + up
    return v.reshape(stores, width)


def widen(w3_ref, w3_wide):
    horizon = w3_ref.shape[0]
    w3_wide[...] = jnp.zeros_like(w3_wide)
    w3_wide[:, :horizon] = w3_ref[...].astype(F32).T.astype(BF16)


def pack_rows(x):
    n = x.shape[0] // 4
    out = x[0:n]
    for k in range(1, 4):
        out = out + pltpu.roll(x[k * n : (k + 1) * n], k * GROUP, axis=1)
    return out


def bottom_kernel(chunk, part, h_ref, w1_ref, w2_ref, w3_ref, pay_ref, item_ref, col_ref, y_ref, w3_wide):
    block, items, days = h_ref.shape
    step = pl.program_id(0)

    @pl.when(step == 0)
    def _():
        widen(w3_ref, w3_wide)
        item_ref[...] = jnp.zeros_like(item_ref)
        col_ref[...] = jnp.zeros_like(col_ref)
        y_ref[...] = jnp.zeros_like(y_ref)

    w1, w2, w3 = w1_ref[...], w2_ref[...], w3_wide[...]
    tiles = days // LANES
    for p in range(block // part):
        x = h_ref[p * part : (p + 1) * part].astype(F32)
        by_store = sum_items(x)
        item_ref[...] += jnp.sum(x, axis=0)
        y = forecaster(x.reshape(part * items, days), w1, w2, w3)
        y_ref[p * part * items : (p + 1) * part * items, :] += pltpu.roll(y, step * GROUP, axis=1)
        y = y.reshape(part, items, LANES)
        row = sum_items(y)
        col_ref[...] += jnp.sum(y, axis=0)
        for q in range(part // chunk):
            peer = p * (part // chunk) + q
            for t in range(tiles):
                pay_ref[peer, t * chunk : (t + 1) * chunk, :] = by_store[
                    q * chunk : (q + 1) * chunk, t * LANES : (t + 1) * LANES
                ]
            pay_ref[peer, tiles * chunk : tiles * chunk + chunk // 4, :] = pack_rows(
                row[q * chunk : (q + 1) * chunk]
            )


def bottom(history, w1, w2, w3, peers, block, part):
    stores, items, days = history.shape
    hid = w1.shape[1]
    rows = stores * items
    chunk = stores // peers
    pay_rows = (days // LANES) * chunk + 8
    fixed = lambda shape: pl.BlockSpec(shape, lambda i: (0,) * len(shape))
    return pl.pallas_call(
        functools.partial(bottom_kernel, chunk, part),
        grid=(stores // block,),
        in_specs=[
            pl.BlockSpec((block, items, days), lambda i: (i, 0, 0)),
            fixed(w1.shape),
            fixed(w2.shape),
            fixed(w3.shape),
        ],
        out_specs=[
            pl.BlockSpec((block // chunk, pay_rows, LANES), lambda i: (i, 0, 0)),
            fixed((items, days)),
            fixed((items, LANES)),
            fixed((block * items, LANES)),
        ],
        out_shape=[
            jax.ShapeDtypeStruct((peers, pay_rows, LANES), F32),
            jax.ShapeDtypeStruct((items, days), F32),
            jax.ShapeDtypeStruct((items, LANES), F32),
            jax.ShapeDtypeStruct((block * items, LANES), F32),
        ],
        scratch_shapes=[pltpu.VMEM((hid, LANES), BF16)],
        compiler_params=params(24),
        cost_estimate=pl.CostEstimate(
            flops=2 * rows * (days * hid + hid * hid + hid * LANES),
            bytes_accessed=2 * history.size,
            transcendentals=0,
        ),
        name="bottom",
    )(stay(history), stay(w1), stay(w2), stay(w3))


def arrange_kernel(horizon, items, y_ref, out_ref):
    block = y_ref.shape[0] // items
    for i in range(items):
        v = y_ref[pl.ds(i, block, stride=items), :].T
        blocks = [v[k * GROUP : k * GROUP + horizon] for k in range(LANES // GROUP)]
        out_ref[i * horizon : (i + 1) * horizon, :] = jnp.concatenate(blocks, axis=1)


def arrange(y, items, horizon):
    rows = y.shape[0]
    stores = rows // items * (LANES // GROUP)
    return pl.pallas_call(
        functools.partial(arrange_kernel, horizon, items),
        in_specs=whole(1),
        out_specs=whole(1)[0],
        out_shape=jax.ShapeDtypeStruct((items * horizon, stores), F32),
        compiler_params=params(12),
        cost_estimate=pl.CostEstimate(
            flops=16 * rows * LANES, bytes_accessed=12 * rows * LANES, transcendentals=0
        ),
        name="arrange",
    )(y)


def totals_kernel(chunk, s_ref, i_ref, w1_ref, w2_ref, w3_ref, col_ref, err_ref, item_ref, pay_ref, w3_wide):
    days = w1_ref.shape[0]
    widen(w3_ref, w3_wide)
    got = s_ref[0]
    for p in range(1, s_ref.shape[0]):
        got = got + s_ref[p]
    tiles = days // LANES
    x = jnp.concatenate([got[t * chunk : (t + 1) * chunk] for t in range(tiles)], axis=1)
    x = jnp.concatenate([x, i_ref[...]], axis=0)
    y = forecaster(x, w1_ref[...], w2_ref[...], w3_wide[...])
    fc = y[:chunk]
    fi = y[chunk:]
    item_ref[...] = fi
    q = chunk // 4
    err_ref[0:q, :] = pack_rows(fc) - got[tiles * chunk : tiles * chunk + q]
    err_ref[q : q + 1, :] = pltpu.roll(jnp.sum(fi, axis=0, keepdims=True), GROUP, axis=1)
    col = col_ref[...]
    sums = jnp.sum(fc, axis=0, keepdims=True) + pltpu.roll(
        jnp.sum(col, axis=0, keepdims=True), 2 * GROUP, axis=1
    )
    packed = pack_rows(col)
    n = packed.shape[0]
    for p in range(pay_ref.shape[0]):
        pay_ref[p, 0:n, :] = packed
        pay_ref[p, n : n + 1, :] = sums


def totals(store_parts, item_hist, w1, w2, w3, col, chunk, item_peers):
    items = item_hist.shape[0]
    return pl.pallas_call(
        functools.partial(totals_kernel, chunk),
        in_specs=whole(6),
        out_specs=whole(3),
        out_shape=[
            jax.ShapeDtypeStruct((8, LANES), F32),
            jax.ShapeDtypeStruct((items, LANES), F32),
            jax.ShapeDtypeStruct((item_peers, 8, LANES), F32),
        ],
        scratch_shapes=[pltpu.VMEM((w1.shape[1], LANES), BF16)],
        compiler_params=params(8),
        name="totals",
    )(store_parts, item_hist, w1, w2, w3, col)


def middle_kernel(chunk, n, err_ref, got_ref, pay_ref):
    q = chunk // 4
    sums = err_ref[q : q + 1, :]
    for p in range(got_ref.shape[0]):
        sums = sums + got_ref[p, n : n + 1, :]
    err = err_ref[0:q, :]
    for p in range(pay_ref.shape[0]):
        pay_ref[p, 0:q, :] = err
        pay_ref[p, q : q + 1, :] = sums


def middle(err, got, chunk, items, peers):
    return pl.pallas_call(
        functools.partial(middle_kernel, chunk, items // 4),
        in_specs=whole(2),
        out_specs=whole(1)[0],
        out_shape=jax.ShapeDtypeStruct((peers, 8, LANES), F32),
        compiler_params=params(2),
        name="middle",
    )(err, got)


def final_kernel(horizon, item_count, store_count, base_ref, item_ref, one_ref, two_ref, out_ref, sgap_ref, igap_ref, err_ref):
    width, stores = base_ref.shape
    items = width // horizon
    peers = two_ref.shape[0]
    valid1 = lax.broadcasted_iota(jnp.int32, (1, LANES), 1) < horizon

    def group(x, k):
        if k:
            x = pltpu.roll(x, LANES - k * GROUP, axis=1)
        return jnp.where(valid1, x, 0.0)

    n = items // 4
    colp = one_ref[0, 0:n, :]
    for p in range(1, one_ref.shape[0]):
        colp = colp + one_ref[p, 0:n, :]
    col = jnp.concatenate([group(colp, k) for k in range(4)], axis=0)
    item_err = item_ref[...] - col

    q = stores // peers // 4
    sums = two_ref[0, q : q + 1, :]
    for p in range(1, peers):
        sums = sums + two_ref[p, q : q + 1, :]
    total = group(sums, 2)
    err_s = group(sums, 0) - total
    err_i = group(sums, 1) - total
    for p in range(peers):
        for k in range(4):
            r = (p * 4 + k) * q
            err_ref[r : r + q, :] = group(two_ref[p, 0:q, :], k)
    store_err = err_ref[...].T[:horizon]

    denominator = 1.0 + item_count + store_count
    shift_s = (err_s * (1.0 + store_count) - store_count * err_i) / denominator
    shift_i = ((1.0 + item_count) * err_i - item_count * err_s) / denominator
    item_shift = (item_err - shift_s) / (1.0 + store_count)
    columns = jnp.concatenate(
        [item_shift, shift_i, jnp.zeros((LANES - items - 1, LANES), F32)], axis=0
    ).T[:horizon]
    store_shift = (store_err - columns[:, items : items + 1]) / (1.0 + item_count)

    a = jnp.concatenate([store_shift, store_shift], axis=0)
    b = jnp.concatenate([columns, pltpu.roll(columns, LANES - 1, axis=1)], axis=0)
    for j in range(items // 2):
        rows = slice(2 * j * horizon, (2 * j + 2) * horizon)
        out_ref[rows, :] = base_ref[rows, :] + a + b[:, 2 * j : 2 * j + 1]
    sgap_ref[...] = store_err * (1.0 / math.sqrt(item_count))
    igap_ref[...] = item_err[:, :horizon] * (1.0 / math.sqrt(store_count))


def final(base, item_fc, one, two, horizon, item_count, store_count):
    width, stores = base.shape
    items = width // horizon
    return pl.pallas_call(
        functools.partial(final_kernel, horizon, item_count, store_count),
        in_specs=whole(4),
        out_specs=whole(3),
        out_shape=[
            jax.ShapeDtypeStruct((width, stores), F32),
            jax.ShapeDtypeStruct((horizon, stores), F32),
            jax.ShapeDtypeStruct((items, horizon), F32),
        ],
        scratch_shapes=[pltpu.VMEM((stores, LANES), F32)],
        compiler_params=params(6),
        name="final",
    )(base, item_fc, one, two)


def exchange(x, axis):
    return lax.all_to_all(x, axis, 0, 0, tiled=True)


def partner(x, axis, flip):
    return lax.ppermute(x, axis, [(i, i ^ flip) for i in range(lax.axis_size(axis))])


def add_over_y(x):
    near, far, across = (partner(x, "store", flip) for flip in (4, 12, 8))
    return (x + across) + (near + far)


def body(history, w1, w2, final_layer_matrix):
    stores, items, _ = history.shape
    horizon = final_layer_matrix.shape[1]
    n_store, n_dept = lax.axis_size("store"), lax.axis_size("dept")
    chunk = stores // n_dept
    w3 = final_layer_matrix.T

    pay, item_part, col, y = bottom(history, w1, w2, w3, n_dept, stores // 4, stores // 8)
    store_parts = exchange(pay, "dept")
    item_hist = add_over_y(item_part + partner(item_part, "store", 1))
    base = arrange(y, items, horizon)
    base, item_hist = lax.optimization_barrier((base, item_hist))
    item_hist = item_hist + partner(item_hist, "store", 2)
    err, item_fc, pay_one = totals(store_parts, item_hist, w1, w2, w3, col, chunk, n_store)
    one = exchange(pay_one, "store")
    pay_two = middle(err, one, chunk, items, n_dept)
    two = exchange(pay_two, "dept")
    out, store_gap, item_gap = final(
        base, item_fc, one, two, horizon, float(items * n_dept), float(stores * n_store)
    )
    return out.T, store_gap, item_gap.T


def solution(mesh):
    return jax.shard_map(
        body,
        mesh=mesh,
        in_specs=(P("store", "dept", None), P(), P(), P()),
        out_specs=(P("store", "dept"), P(None, "store"), P(None, "dept")),
        check_vma=False,
    )
```

```python
import functools
import math

import jax
import jax.numpy as jnp
from jax import lax
from jax.experimental import pallas as pl
from jax.experimental.pallas import tpu as pltpu
from jax.sharding import PartitionSpec as P

F32 = jnp.float32
BF16 = jnp.bfloat16
LANES = 128
GROUP = 32
MIB = 1024 * 1024


def whole(n):
    return [pl.BlockSpec(memory_space=pltpu.VMEM)] * n


def params(mib):
    return pltpu.CompilerParams(vmem_limit_bytes=mib * MIB)


def stay(x):
    return pltpu.with_memory_space_constraint(x, pltpu.HBM)


def relu(x):
    return jnp.maximum(x.astype(BF16), 0)


def forecaster(x, w1, w2, w3):
    var = jnp.sum(x * x, axis=-1, keepdims=True) * (1.0 / x.shape[-1]) + 1e-05
    inv = lax.rsqrt(var)
    z = (x * inv).astype(BF16)
    a = relu(jnp.dot(z, w1, preferred_element_type=F32))
    b = relu(jnp.dot(a, w2, preferred_element_type=F32))
    return jnp.dot(b, w3, preferred_element_type=F32) * (var * inv)


def sum_items(x):
    stores, items, width = x.shape
    x = x.reshape(stores, items // 8, 8, width)
    total = x[:, 0]
    for k in range(1, items // 8):
        total = total + x[:, k]
    v = total.reshape(stores // 8, 8, 8, width)
    row = lax.broadcasted_iota(jnp.int32, (1, 1, 8, width), 2)
    for bit in (4, 2, 1):
        low = lax.rem(lax.div(row, bit), 2) == 0
        a, b = v[:, :bit], v[:, bit:]
        there = jnp.where(low, b, a)
        up = pltpu.roll(there, bit, axis=2)
        if bit < 4:
            up = jnp.where(low, pltpu.roll(there, 8 - bit, axis=2), up)
        v = jnp.where(low, a, b) + up
    return v.reshape(stores, width)


def widen(w3_ref, w3_wide):
    horizon = w3_ref.shape[0]
    w3_wide[...] = jnp.zeros_like(w3_wide)
    w3_wide[:, :horizon] = w3_ref[...].astype(F32).T.astype(BF16)


def pack_rows(x):
    n = x.shape[0] // 4
    out = x[0:n]
    for k in range(1, 4):
        out = out + pltpu.roll(x[k * n : (k + 1) * n], k * GROUP, axis=1)
    return out


def bottom_kernel(chunk, part, h_ref, w1_ref, w2_ref, w3_ref, pay_ref, item_ref, col_ref, y_ref, w3_wide):
    block, items, days = h_ref.shape
    step = pl.program_id(0)

    @pl.when(step == 0)
    def _():
        widen(w3_ref, w3_wide)
        item_ref[...] = jnp.zeros_like(item_ref)
        col_ref[...] = jnp.zeros_like(col_ref)
        y_ref[...] = jnp.zeros_like(y_ref)

    w1, w2, w3 = w1_ref[...], w2_ref[...], w3_wide[...]
    tiles = days // LANES
    for p in range(block // part):
        x = h_ref[p * part : (p + 1) * part].astype(F32)
        by_store = sum_items(x)
        item_ref[...] += jnp.sum(x, axis=0)
        y = forecaster(x.reshape(part * items, days), w1, w2, w3)
        y_ref[p * part * items : (p + 1) * part * items, :] += pltpu.roll(y, step * GROUP, axis=1)
        y = y.reshape(part, items, LANES)
        row = sum_items(y)
        col_ref[...] += jnp.sum(y, axis=0)
        for q in range(part // chunk):
            peer = p * (part // chunk) + q
            for t in range(tiles):
                pay_ref[peer, t * chunk : (t + 1) * chunk, :] = by_store[
                    q * chunk : (q + 1) * chunk, t * LANES : (t + 1) * LANES
                ]
            pay_ref[peer, tiles * chunk : tiles * chunk + chunk // 4, :] = pack_rows(
                row[q * chunk : (q + 1) * chunk]
            )


def bottom(history, w1, w2, w3, peers, block, part):
    stores, items, days = history.shape
    hid = w1.shape[1]
    rows = stores * items
    chunk = stores // peers
    pay_rows = (days // LANES) * chunk + 8
    fixed = lambda shape: pl.BlockSpec(shape, lambda i: (0,) * len(shape))
    return pl.pallas_call(
        functools.partial(bottom_kernel, chunk, part),
        grid=(stores // block,),
        in_specs=[
            pl.BlockSpec((block, items, days), lambda i: (i, 0, 0)),
            fixed(w1.shape),
            fixed(w2.shape),
            fixed(w3.shape),
        ],
        out_specs=[
            pl.BlockSpec((block // chunk, pay_rows, LANES), lambda i: (i, 0, 0)),
            fixed((items, days)),
            fixed((items, LANES)),
            fixed((block * items, LANES)),
        ],
        out_shape=[
            jax.ShapeDtypeStruct((peers, pay_rows, LANES), F32),
            jax.ShapeDtypeStruct((items, days), F32),
            jax.ShapeDtypeStruct((items, LANES), F32),
            jax.ShapeDtypeStruct((block * items, LANES), F32),
        ],
        scratch_shapes=[pltpu.VMEM((hid, LANES), BF16)],
        compiler_params=params(24),
        cost_estimate=pl.CostEstimate(
            flops=2 * rows * (days * hid + hid * hid + hid * LANES),
            bytes_accessed=2 * history.size,
            transcendentals=0,
        ),
        name="bottom",
    )(stay(history), stay(w1), stay(w2), stay(w3))


def arrange_kernel(horizon, items, y_ref, out_ref):
    block = y_ref.shape[0] // items
    for i in range(items):
        v = y_ref[pl.ds(i, block, stride=items), :].T
        blocks = [v[k * GROUP : k * GROUP + horizon] for k in range(LANES // GROUP)]
        out_ref[i * horizon : (i + 1) * horizon, :] = jnp.concatenate(blocks, axis=1)


def arrange(y, items, horizon):
    rows = y.shape[0]
    stores = rows // items * (LANES // GROUP)
    return pl.pallas_call(
        functools.partial(arrange_kernel, horizon, items),
        in_specs=whole(1),
        out_specs=whole(1)[0],
        out_shape=jax.ShapeDtypeStruct((items * horizon, stores), F32),
        compiler_params=params(12),
        cost_estimate=pl.CostEstimate(
            flops=16 * rows * LANES, bytes_accessed=12 * rows * LANES, transcendentals=0
        ),
        name="arrange",
    )(y)


def totals_kernel(chunk, s_ref, i_ref, w1_ref, w2_ref, w3_ref, col_ref, err_ref, item_ref, pay_ref, w3_wide):
    days = w1_ref.shape[0]
    widen(w3_ref, w3_wide)
    got = s_ref[0]
    for p in range(1, s_ref.shape[0]):
        got = got + s_ref[p]
    tiles = days // LANES
    x = jnp.concatenate([got[t * chunk : (t + 1) * chunk] for t in range(tiles)], axis=1)
    x = jnp.concatenate([x, i_ref[...]], axis=0)
    y = forecaster(x, w1_ref[...], w2_ref[...], w3_wide[...])
    fc = y[:chunk]
    fi = y[chunk:]
    item_ref[...] = fi
    q = chunk // 4
    err_ref[0:q, :] = pack_rows(fc) - got[tiles * chunk : tiles * chunk + q]
    err_ref[q : q + 1, :] = pltpu.roll(jnp.sum(fi, axis=0, keepdims=True), GROUP, axis=1)
    col = col_ref[...]
    sums = jnp.sum(fc, axis=0, keepdims=True) + pltpu.roll(
        jnp.sum(col, axis=0, keepdims=True), 2 * GROUP, axis=1
    )
    packed = pack_rows(col)
    n = packed.shape[0]
    for p in range(pay_ref.shape[0]):
        pay_ref[p, 0:n, :] = packed
        pay_ref[p, n : n + 1, :] = sums


def totals(store_parts, item_hist, w1, w2, w3, col, chunk, item_peers):
    items = item_hist.shape[0]
    return pl.pallas_call(
        functools.partial(totals_kernel, chunk),
        in_specs=whole(6),
        out_specs=whole(3),
        out_shape=[
            jax.ShapeDtypeStruct((8, LANES), F32),
            jax.ShapeDtypeStruct((items, LANES), F32),
            jax.ShapeDtypeStruct((item_peers, 8, LANES), F32),
        ],
        scratch_shapes=[pltpu.VMEM((w1.shape[1], LANES), BF16)],
        compiler_params=params(8),
        name="totals",
    )(store_parts, item_hist, w1, w2, w3, col)


def middle_kernel(chunk, n, err_ref, got_ref, pay_ref):
    q = chunk // 4
    sums = err_ref[q : q + 1, :]
    for p in range(got_ref.shape[0]):
        sums = sums + got_ref[p, n : n + 1, :]
    err = err_ref[0:q, :]
    for p in range(pay_ref.shape[0]):
        pay_ref[p, 0:q, :] = err
        pay_ref[p, q : q + 1, :] = sums


def middle(err, got, chunk, items, peers):
    return pl.pallas_call(
        functools.partial(middle_kernel, chunk, items // 4),
        in_specs=whole(2),
        out_specs=whole(1)[0],
        out_shape=jax.ShapeDtypeStruct((peers, 8, LANES), F32),
        compiler_params=params(2),
        name="middle",
    )(err, got)


def final_kernel(horizon, item_count, store_count, base_ref, item_ref, one_ref, two_ref, out_ref, sgap_ref, igap_ref, err_ref):
    width, stores = base_ref.shape
    items = width // horizon
    peers = two_ref.shape[0]
    valid1 = lax.broadcasted_iota(jnp.int32, (1, LANES), 1) < horizon

    def group(x, k):
        if k:
            x = pltpu.roll(x, LANES - k * GROUP, axis=1)
        return jnp.where(valid1, x, 0.0)

    n = items // 4
    colp = one_ref[0, 0:n, :]
    for p in range(1, one_ref.shape[0]):
        colp = colp + one_ref[p, 0:n, :]
    col = jnp.concatenate([group(colp, k) for k in range(4)], axis=0)
    item_err = item_ref[...] - col

    q = stores // peers // 4
    sums = two_ref[0, q : q + 1, :]
    for p in range(1, peers):
        sums = sums + two_ref[p, q : q + 1, :]
    total = group(sums, 2)
    err_s = group(sums, 0) - total
    err_i = group(sums, 1) - total
    for p in range(peers):
        for k in range(4):
            r = (p * 4 + k) * q
            err_ref[r : r + q, :] = group(two_ref[p, 0:q, :], k)
    store_err = err_ref[...].T[:horizon]

    denominator = 1.0 + item_count + store_count
    shift_s = (err_s * (1.0 + store_count) - store_count * err_i) / denominator
    shift_i = ((1.0 + item_count) * err_i - item_count * err_s) / denominator
    item_shift = (item_err - shift_s) / (1.0 + store_count)
    columns = jnp.concatenate(
        [item_shift, shift_i, jnp.zeros((LANES - items - 1, LANES), F32)], axis=0
    ).T[:horizon]
    store_shift = (store_err - columns[:, items : items + 1]) / (1.0 + item_count)

    a = jnp.concatenate([store_shift, store_shift], axis=0)
    b = jnp.concatenate([columns, pltpu.roll(columns, LANES - 1, axis=1)], axis=0)
    for j in range(items // 2):
        rows = slice(2 * j * horizon, (2 * j + 2) * horizon)
        out_ref[rows, :] = base_ref[rows, :] + a + b[:, 2 * j : 2 * j + 1]
    sgap_ref[...] = store_err * (1.0 / math.sqrt(item_count))
    igap_ref[...] = item_err[:, :horizon] * (1.0 / math.sqrt(store_count))


def final(base, item_fc, one, two, horizon, item_count, store_count):
    width, stores = base.shape
    items = width // horizon
    return pl.pallas_call(
        functools.partial(final_kernel, horizon, item_count, store_count),
        in_specs=whole(4),
        out_specs=whole(3),
        out_shape=[
            jax.ShapeDtypeStruct((width, stores), F32),
            jax.ShapeDtypeStruct((horizon, stores), F32),
            jax.ShapeDtypeStruct((items, horizon), F32),
        ],
        scratch_shapes=[pltpu.VMEM((stores, LANES), F32)],
        compiler_params=params(6),
        name="final",
    )(base, item_fc, one, two)


def exchange(x, axis):
    return lax.all_to_all(x, axis, 0, 0, tiled=True)


def partner(x, axis, flip):
    return lax.ppermute(x, axis, [(i, i ^ flip) for i in range(lax.axis_size(axis))])


def add_over_x(x):
    x = x + partner(x, "store", 1)
    return x + partner(x, "store", 2)


def add_over_y(x):
    x = x + partner(x, "store", 4)
    return x + partner(x, "store", 12)


def body(history, w1, w2, final_layer_matrix):
    stores, items, _ = history.shape
    horizon = final_layer_matrix.shape[1]
    n_store, n_dept = lax.axis_size("store"), lax.axis_size("dept")
    chunk = stores // n_dept
    w3 = final_layer_matrix.T

    pay, item_part, col, y = bottom(history, w1, w2, w3, n_dept, stores // 4, stores // 8)
    store_parts = exchange(pay, "dept")
    item_hist = add_over_x(item_part)
    base = arrange(y, items, horizon)
    base, item_hist = lax.optimization_barrier((base, item_hist))
    item_hist = add_over_y(item_hist)
    err, item_fc, pay_one = totals(store_parts, item_hist, w1, w2, w3, col, chunk, n_store)
    one = exchange(pay_one, "store")
    pay_two = middle(err, one, chunk, items, n_dept)
    two = exchange(pay_two, "dept")
    out, store_gap, item_gap = final(
        base, item_fc, one, two, horizon, float(items * n_dept), float(stores * n_store)
    )
    return out.T, store_gap, item_gap.T


def solution(mesh):
    return jax.shard_map(
        body,
        mesh=mesh,
        in_specs=(P("store", "dept", None), P(), P(), P()),
        out_specs=(P("store", "dept"), P(None, "store"), P(None, "dept")),
        check_vma=False,
    )
```
